32 devices in a mesh: row: 4 (over z), col: 2 (over x), feat: 4 (over y, core).
Axes of the slice: x: 2, y: 2, z: 4, core: 2. Of those that a mesh axis runs over, the one named last changes fastest.
Arguments:
- snapshots: bfloat16 [512, 32768], P(('row', 'col'), 'feat'), may hold values from -6 to 6
- start_block: float32 [512, 32], P('row'), may hold values from -6 to 6
Outputs:
- eigen_basis: float32 [512, 32], P('row')
The draws below stay inside these ranges and needn't reach their ends.
All inputs are finite; a program needn't handle non-finite values.
Results may differ from the reference program's by a relative error of at most 0.0003.
Values may be sent and summed in bfloat16 or wider, within the bound.
No kernel may reach another device: no remote copies, remote signals or barrier semaphores. Data moves between devices by JAX's collectives and lax.ppermute only.
A program may use at most 64 MiB of HBM per device.

```python
import math
import jax
import jax.numpy as jnp
from jax import lax

BLOCK = 128
PTS = 32768
LAGS = 128
VECS = 32
ITERS = 6
SNAPS = 512


def draw_snapshots(key, part):
    keys = jax.random.split(key, 9)
    period = BLOCK * 10.0 / 7.0
    duration = period / 2.0
    event_count = max(2, SNAPS // (2 * BLOCK))
    amp_low = 0.2
    amp_high = 3.0
    innovations = jax.random.normal(keys[0], (SNAPS, PTS), jnp.float32)
    noise = jax.random.normal(keys[1], (SNAPS, PTS), jnp.float32)
    event_gain = 1.5
    amplitude = jnp.exp(jax.random.uniform(keys[2], (PTS,), jnp.float32, math.log(amp_low), math.log(amp_high)))
    amplitude = amplitude / jnp.sqrt(jnp.mean(amplitude * amplitude))
    phase = jax.random.uniform(keys[3], (PTS,), jnp.float32, -math.pi, math.pi)
    horizon = jnp.exp(jax.random.uniform(keys[4], (PTS,), jnp.float32, math.log(BLOCK / 50.0), math.log(2.0 * BLOCK)))
    memory = jnp.exp(-1.0 / horizon)
    drive = jnp.sqrt(1.0 - memory * memory)
    begin = jax.random.normal(keys[5], (PTS,), jnp.float32)

    def advance(state, innovation):
        fresh = memory * state + drive * innovation
        return (fresh, fresh)
    unused, anomaly = lax.scan(advance, begin, innovations)
    times = jnp.arange(SNAPS, dtype=jnp.float32)
    starts = jax.random.uniform(keys[6], (event_count,), jnp.float32, -duration, float(SNAPS))
    offset = times[:, None] - starts[None, :]
    inside = jnp.logical_and(offset >= 0.0, offset < duration)
    bump = jnp.where(inside, jnp.sin(math.pi * offset / duration) ** 2, 0.0)
    centres = jax.random.uniform(keys[7], (event_count,), jnp.float32, 0.0, float(PTS))
    points = jnp.arange(PTS, dtype=jnp.float32)
    distance_along = jnp.mod(points[None, :] - centres[:, None], float(PTS))
    patch = (distance_along < PTS / 8.0).astype(jnp.float32)
    strength = jnp.exp(jax.random.uniform(keys[8], (event_count, PTS), jnp.float32, math.log(0.5), math.log(2.0)))
    pattern = patch * strength
    event_term = jnp.dot(bump, pattern, precision=lax.Precision.HIGHEST)
    envelope = 1.0 + jnp.sum(bump, axis=1)
    cycle = math.sqrt(2.0) * jnp.cos(2.0 * math.pi * times[:, None] / period + phase[None, :])
    core = math.sqrt(0.6) * cycle + math.sqrt(0.25) * envelope[:, None] * anomaly + math.sqrt(0.15) * noise
    field = amplitude[None, :] * core + event_gain * event_term
    return jnp.clip(field, -6.0, 6.0).astype(jnp.bfloat16)


def block_levels(own_key, extent, cuts, least, high):
    loudness = 1.0
    for axis_at, blocks in cuts:
        heights = jax.random.uniform(jax.random.fold_in(jax.random.fold_in(own_key, 6), axis_at), (blocks,), jnp.float32, least / len(cuts), high / len(cuts))
        loudness = loudness * jnp.repeat(jnp.exp(heights), extent[axis_at] // blocks).reshape((-1,) + (1,) * (len(extent) - 1 - axis_at))
    return loudness


def bell_draw(key, shape, width, bound, cuts=(), kind=jnp.bfloat16):
    array = jax.random.normal(key, shape, jnp.float32) * width
    if len(cuts) > 0:
        array = block_levels(key, shape, cuts, -0.22, 0.18) * array
    return jnp.clip(array, min=-bound, max=bound).astype(kind)


def setup_inputs(seed: int = 0) -> dict:
    seeds = jax.random.split(jax.random.key(seed), 3)
    return {
        "snapshots": draw_snapshots(jax.random.fold_in(seeds[2], 71), 0),
        "start_block": bell_draw(seeds[1], (SNAPS, VECS), 1.0, 6.0, ((0, 4),), jnp.float32),
    }


kernel_spread = 0.25
highest = lax.Precision.HIGHEST

def lag_window(distance):
    rim = LAGS - 1
    padded = jnp.pad(distance, ((rim, 0), (rim, 0)))
    running = jnp.zeros_like(distance)
    size_now = distance.shape[0]
    for lag_index in range(LAGS):
        begin = rim - lag_index
        running = running + padded[begin:begin + size_now, begin:begin + size_now]
    return running

def reference(snapshots, start_block):
    field = snapshots.astype(jnp.float32)
    norms = lax.optimization_barrier(jnp.sum(field * field, axis=1))
    gram = jnp.dot(field.astype(jnp.float32), field.T.astype(jnp.float32), precision=highest, preferred_element_type=jnp.float32)
    distance = norms[:, None] + norms[None, :] - 2.0 * gram
    lagged = lag_window(distance)
    idents = jnp.arange(SNAPS, dtype=jnp.int32)
    counts = jnp.minimum(jnp.minimum(idents[:, None], idents[None, :]), LAGS - 1) + 1
    kernel = jnp.exp(-(lagged / (counts.astype(jnp.float32) * PTS)) / kernel_spread)
    degrees = lax.optimization_barrier(jnp.sum(kernel, axis=1))
    scales = lax.rsqrt(degrees)
    markov = kernel * scales[:, None] * scales[None, :]
    basis = start_block
    for rounds in range(ITERS):
        product = jnp.dot(markov.astype(jnp.float32), basis.astype(jnp.float32), precision=highest, preferred_element_type=jnp.float32)
        small = jnp.dot(product.T.astype(jnp.float32), product.astype(jnp.float32), precision=highest, preferred_element_type=jnp.float32)
        factor = jnp.linalg.cholesky(small)
        basis = jax.scipy.linalg.solve_triangular(factor, product.T, lower=True).T
    return basis * math.sqrt(SNAPS)
```

```python
import functools
import math

import jax
import jax.numpy as jnp
from jax import lax
from jax.experimental import pallas as pl
from jax.experimental.pallas import tpu as pltpu
from jax.sharding import PartitionSpec as P

LAGS = 128
ITERS = 6
TILE = 128


kernel_spread = 0.25
highest = lax.Precision.HIGHEST
f32 = jnp.float32
bf16 = jnp.bfloat16


def broadcast(x, axis, root):
    mine = lax.axis_index(axis) == root
    return lax.psum(jnp.where(mine, x, jnp.zeros_like(x)), axis)


def shifted(x, axis, by):
    length = lax.axis_size(axis)
    pairs = [(i, i + by) for i in range(length) if 0 <= i + by < length]
    return lax.ppermute(x, axis, pairs)


def diagonal_window(extended, lag_count):
    running = None
    offset = 0
    partial_sum = extended
    levels = lag_count.bit_length()
    for level in range(levels):
        stride = 1 << level
        if lag_count & stride:
            running = partial_sum
            offset = offset + stride
        if level + 1 < levels:
            partial_sum = partial_sum[:-stride, :-stride] + partial_sum[stride:, stride:]
    return running


def orthonormal(product, gram_sum):
    factor = jnp.linalg.cholesky(gram_sum)
    return jax.scipy.linalg.solve_triangular(factor, product.T, lower=True).T


def square_norms(fields):
    widened = fields.astype(f32)
    return jnp.sum(widened * widened, axis=1)


def spread_body(points, snapshots, start_block):
    row_total = lax.axis_size("row")
    col_total = lax.axis_size("col")
    row_place = lax.axis_index("row")
    col_place = lax.axis_index("col")
    shard_rows = snapshots.shape[0]
    block_rows = shard_rows * col_total
    pairing = row_total // col_total
    block_cols = block_rows * pairing
    own_rows = lax.all_gather(snapshots, "col", axis=0, tiled=True)
    own_norms = square_norms(own_rows)
    members = []
    for member in range(pairing):
        members.append(broadcast(own_rows, "row", pairing * col_place + member))
    col_data = jnp.concatenate(members, axis=0)
    col_norms = square_norms(col_data)
    products = lax.dot_general(
        own_rows, col_data, (((1,), (1,)), ((), ())), preferred_element_type=f32
    )
    partial_dist = own_norms[:, None] + col_norms[None, :] - 2.0 * products
    distance = lax.psum(partial_dist, "feat")
    rim_width = LAGS - 1
    top_rim = shifted(distance[block_rows - rim_width :], "row", 1)
    upper = jnp.concatenate([top_rim, distance], axis=0)
    left_side = shifted(upper[:, block_cols - rim_width :], "col", 1)
    extended = jnp.concatenate([left_side, upper], axis=1)
    lagged = diagonal_window(extended, LAGS)
    row_ids = row_place * block_rows + lax.broadcasted_iota(jnp.int32, (block_rows, block_cols), 0)
    col_ids = col_place * block_cols + lax.broadcasted_iota(jnp.int32, (block_rows, block_cols), 1)
    counts = jnp.minimum(jnp.minimum(row_ids, col_ids), rim_width) + 1
    kernel = jnp.exp(-(lagged / (counts.astype(f32) * points)) / kernel_spread)
    row_degree = lax.psum(jnp.sum(kernel, axis=1), "col")
    every_degree = lax.all_gather(row_degree, "row", axis=0, tiled=True)
    col_degree = lax.dynamic_slice_in_dim(every_degree, col_place * block_cols, block_cols)
    markov = kernel * lax.rsqrt(row_degree)[:, None] * lax.rsqrt(col_degree)[None, :]
    basis = start_block
    for rounds in range(ITERS // 2):
        product = lax.dot_general(
            markov,
            basis,
            (((0,), (0,)), ((), ())),
            precision=highest,
            preferred_element_type=f32,
        )
        summed_cols = lax.psum(product, "row")
        row_product = jnp.dot(markov, summed_cols, precision=highest, preferred_element_type=f32)
        summed_rows = lax.psum(row_product, "col")
        local_gram = jnp.dot(
            summed_rows.T, summed_rows, precision=highest, preferred_element_type=f32
        )
        gram_rows = lax.psum(local_gram, "row")
        basis = orthonormal(summed_rows, gram_rows)
    return basis * math.sqrt(row_total * block_rows)


def any_spec():
    return pl.BlockSpec(memory_space=pl.ANY)


def smem_spec():
    return pl.BlockSpec(memory_space=pltpu.SMEM)


def vmem_spec():
    return pl.BlockSpec(memory_space=pltpu.VMEM)


def xor_permute(x, axis, mask):
    return lax.ppermute(x, axis, [(i, i ^ mask) for i in range(lax.axis_size(axis))])


def quad_permute(x, mask):
    cols, feats = lax.axis_size("col"), lax.axis_size("feat")
    pairs = []
    for col in range(cols):
        for feat in range(feats):
            there = (col ^ (mask >> 1)) * feats + (feat ^ ((mask & 1) * (feats // 2)))
            pairs.append((col * feats + feat, there))
    return lax.ppermute(x, ("col", "feat"), pairs)


def packed_blocks(tiles):
    return [(b, c) for b in range(tiles) for c in range(tiles - b)]


def cut_kernel(members, width, place_ref, x_ref, *refs):
    outs, sems = refs[: members - 1], refs[members - 1]
    me = place_ref[0]
    copies = []
    for step in range(1, members):
        begin = pl.multiple_of((me ^ step) * width, TILE)
        copies.append(
            pltpu.make_async_copy(x_ref.at[:, pl.ds(begin, width)], outs[step - 1], sems.at[step - 1])
        )
    for copy in copies:
        copy.start()
    for copy in copies:
        copy.wait()


def gram_kernel(members, rows, width, place_ref, x_ref, *refs):
    received = refs[: members - 1]
    keep_ref, send_ref, data_ref, sems = refs[members - 1 :]
    me, half = place_ref[0], place_ref[1]
    copies = []
    for step in range(members):
        if step == 0:
            source = x_ref.at[:, pl.ds(pl.multiple_of(me * width, TILE), width)]
        else:
            source = received[step - 1]
        begin = pl.multiple_of((me ^ step) * rows, rows)
        copies.append(pltpu.make_async_copy(source, data_ref.at[pl.ds(begin, rows), :], sems.at[step]))
    for copy in copies:
        copy.start()
    for copy in copies:
        copy.wait()
    tiles = members * rows // TILE
    sub = lax.broadcasted_iota(jnp.int32, (TILE, TILE), 0)
    lane = lax.broadcasted_iota(jnp.int32, (TILE, TILE), 1)
    anti = sub + lane == TILE - 1
    flip = anti.astype(bf16)
    contract = (((1,), (1,)), ((), ()))
    strips, row_norms, col_norms = [], [], []
    for b in range(tiles):
        mirror = tiles - 1 - b
        block = data_ref[mirror * TILE : (mirror + 1) * TILE, :]
        turned = jnp.dot(flip, block, preferred_element_type=f32).astype(bf16)
        prods = lax.dot_general(
            turned, data_ref[: (mirror + 1) * TILE, :], contract, preferred_element_type=f32
        )
        strips.append(prods)
        own = jnp.where(anti, prods[:, mirror * TILE :], 0.0)
        row_norms.append(jnp.sum(own, axis=1, keepdims=True))
        col_norms.append(jnp.sum(own, axis=0, keepdims=True))
    norms = jnp.concatenate(col_norms[::-1], axis=1)
    total = len(packed_blocks(tiles))
    at = 0
    for b in range(tiles):
        span = (tiles - b) * TILE
        dist = row_norms[b] + norms[:, :span] - 2.0 * strips[b]
        turned = pltpu.roll(dist, 0, 1, stride=1, stride_axis=0)
        head = jnp.where(lane >= sub, turned[:, :TILE], 0.0)
        for c in range(tiles - b):
            value = head if c == 0 else turned[:, c * TILE : (c + 1) * TILE]
            side, slot = at // (total // 2), at % (total // 2)

            @pl.when(half == side)
            def _(value=value, slot=slot):
                keep_ref[slot * TILE : (slot + 1) * TILE, :] = value

            @pl.when(half != side)
            def _(value=value, slot=slot):
                send_ref[slot * TILE : (slot + 1) * TILE, :] = value

            at += 1


def quarter_kernel(chunk, place_ref, keep_ref, got_ref, *outs):
    quad = place_ref[2]
    for mask in range(4):
        rows = pl.ds(pl.multiple_of((quad ^ mask) * chunk, 8), chunk)
        outs[mask][...] = keep_ref[rows, :] + got_ref[rows, :]


def split(x):
    high = x.astype(bf16)
    return high, (x - high.astype(f32)).astype(bf16)


def split_dot(a, b, contract=(((1,), (0,)), ((), ()))):
    a_high, a_low = split(a)
    b_high, b_low = split(b)
    rows = a.shape[0]
    stacked = jnp.concatenate([a_high, a_low], axis=0)
    first = lax.dot_general(stacked, b_high, contract, preferred_element_type=f32)
    second = lax.dot_general(a_high, b_low, contract, preferred_element_type=f32)
    return first[:rows] + (first[rows:] + second)


def inverse_factor(small):
    size = small.shape[0]
    sub = lax.broadcasted_iota(jnp.int32, (size, size), 0)
    lane = lax.broadcasted_iota(jnp.int32, (size, size), 1)
    eye = (sub == lane).astype(f32)
    work = jnp.concatenate([small, eye], axis=1)
    below = lax.broadcasted_iota(jnp.int32, (size, 1), 0)
    for k in range(size - 1):
        row = work[k : k + 1, :]
        scale = work[:, k : k + 1] / work[k : k + 1, k : k + 1]
        work = work - jnp.where(below > k, scale, 0.0) * row
    pivots = jnp.sum(work[:, :size] * eye, axis=1, keepdims=True)
    begin = jnp.sum(small * eye, axis=1, keepdims=True)
    return work[:, size:] * lax.rsqrt(pivots), jnp.min(pivots / begin)


def finish_kernel(points, tiles, chunk, snaps, place_ref, *refs):
    pieces = refs[:8]
    starts = refs[8:12]
    out_ref, packed_ref, high_ref, low_ref, start_ref, wide_ref, sems = refs[12:]
    half, quad, row_place = place_ref[1], place_ref[2], place_ref[3]
    copies = []
    for side in range(2):
        for mask in range(4):
            begin = pl.multiple_of((half ^ side) * (4 * chunk) + (quad ^ mask) * chunk, 8)
            copies.append(
                pltpu.make_async_copy(
                    pieces[side * 4 + mask],
                    packed_ref.at[pl.ds(begin, chunk), :],
                    sems.at[side * 4 + mask],
                )
            )
    rows = snaps // 4
    for mask in range(4):
        begin = pl.multiple_of((row_place ^ mask) * rows, 8)
        copies.append(
            pltpu.make_async_copy(
                starts[mask], start_ref.at[pl.ds(begin, rows), :], sems.at[8 + mask]
            )
        )
    for copy in copies:
        copy.start()
    for copy in copies:
        copy.wait()
    sub = lax.broadcasted_iota(jnp.int32, (TILE, TILE), 0)
    lane = lax.broadcasted_iota(jnp.int32, (TILE, TILE), 1)
    late = (sub + lane >= TILE - 1).astype(bf16)
    early = (sub + lane < TILE - 1).astype(bf16)
    places = {}
    for at, (b, c) in enumerate(packed_blocks(tiles)):
        places[(b, b + c)] = at

    def strip(b, first):
        parts = []
        for c in range(first, tiles):
            at = places[(b, c)]
            parts.append(packed_ref[at * TILE : (at + 1) * TILE, :])
        whole = jnp.concatenate(parts, axis=1) if len(parts) > 1 else parts[0]
        high = whole.astype(bf16)
        rest = whole - high.astype(f32)
        middle = rest.astype(bf16)
        low = (rest - middle.astype(f32)).astype(bf16)
        return high, middle, low

    strips = [strip(b, b) for b in range(tiles)]
    for block in range(tiles):
        b = tiles - 1 - block
        span = (block + 1) * TILE
        lagged = None
        for piece in strips[b]:
            term = jnp.dot(late, piece, preferred_element_type=f32)
            lagged = term if lagged is None else lagged + term
        if block > 0:
            more = None
            for piece in strips[b + 1]:
                term = jnp.dot(early, piece, preferred_element_type=f32)
                more = term if more is None else more + term
            lagged = jnp.concatenate([lagged[:, :TILE], lagged[:, TILE:] + more], axis=1)
        lagged = pltpu.roll(lagged, (1 + span - TILE) % span, 1, stride=1, stride_axis=0)
        columns = lax.broadcasted_iota(jnp.int32, (1, span), 1)
        counts = (jnp.minimum(columns, LAGS - 1) + 1).astype(f32)
        kernel = jnp.exp(lagged * (-1.0 / (counts * (points * kernel_spread))))
        for c in range(block + 1):
            value = kernel[:, c * TILE : (c + 1) * TILE]
            if c == block:
                value = jnp.where(lane <= sub, value, value.T)
            high, low = split(value)
            high_ref[block * TILE : (block + 1) * TILE, c * TILE : (c + 1) * TILE] = high
            low_ref[block * TILE : (block + 1) * TILE, c * TILE : (c + 1) * TILE] = low
            if c < block:
                high, low = split(value.T)
                high_ref[c * TILE : (c + 1) * TILE, block * TILE : (block + 1) * TILE] = high
                low_ref[c * TILE : (c + 1) * TILE, block * TILE : (block + 1) * TILE] = low
    ones = jnp.ones((16, snaps), bf16)
    degrees = jnp.dot(ones, high_ref[...], preferred_element_type=f32)
    degrees = degrees + jnp.dot(ones, low_ref[...], preferred_element_type=f32)
    inverse = 1.0 / degrees[0:1, :]
    scales = lax.sqrt(inverse)
    vecs = start_ref.shape[1]
    start = jnp.concatenate(
        [start_ref[b * TILE : (b + 1) * TILE, :].T for b in range(tiles)], axis=1
    )

    def apply(x):
        x_high, x_low = split(x)
        stacked = jnp.concatenate([x_high, x_low], axis=0)
        first = jnp.dot(stacked, high_ref[...], preferred_element_type=f32)
        second = jnp.dot(x_high, low_ref[...], preferred_element_type=f32)
        return first[:vecs] + (first[vecs:] + second)

    across = (((1,), (1,)), ((), ()))

    def rounds(x, least, times):
        x = apply(x * scales)
        for _ in range(times - 1):
            x = apply(x * inverse)
        x = x * scales
        factor, ratio = inverse_factor(split_dot(x, x, across))
        return split_dot(factor, x), jnp.minimum(least, ratio)

    def loop(times):
        return lax.fori_loop(
            0, ITERS // times, lambda _, c: rounds(c[0], c[1], times), (start, f32(1.0))
        )

    basis, least = loop(3)
    wide_ref[...] = basis

    @pl.when(jnp.logical_not(least > 1e-4))
    def _():
        wide_ref[...] = loop(1)[0]

    basis = wide_ref[...]
    eye_sub = lax.broadcasted_iota(jnp.int32, (vecs, vecs), 0)
    eye_lane = lax.broadcasted_iota(jnp.int32, (vecs, vecs), 1)
    error = split_dot(basis, basis, across) - (eye_sub == eye_lane).astype(f32)
    weight = jnp.where(eye_sub > eye_lane, 1.0, jnp.where(eye_sub == eye_lane, 0.5, 0.0))
    wide_ref[...] = (basis - split_dot(error * weight, basis)) * math.sqrt(snaps)
    own = wide_ref[:, pl.ds(pl.multiple_of(row_place * rows, TILE), rows)]
    out_ref[...] = own.T


def packed_body(points, snapshots, start_block):
    cols, feats = lax.axis_size("col"), lax.axis_size("feat")
    rows_total = lax.axis_size("row")
    members = rows_total * cols
    shard_rows, shard_points = snapshots.shape
    width = shard_points // members
    snaps = shard_rows * members
    tiles = snaps // TILE
    vecs = start_block.shape[1]
    row_place, col_place = lax.axis_index("row"), lax.axis_index("col")
    feat_place = lax.axis_index("feat")
    me = row_place * cols + col_place
    half = feat_place % 2
    quad = col_place * 2 + feat_place // 2
    place = jnp.stack([me, half, quad, row_place]).astype(jnp.int32)

    cuts = pl.pallas_call(
        functools.partial(cut_kernel, members, width),
        out_shape=[jax.ShapeDtypeStruct((shard_rows, width), bf16)] * (members - 1),
        in_specs=[smem_spec(), any_spec()],
        out_specs=[any_spec()] * (members - 1),
        scratch_shapes=[pltpu.SemaphoreType.DMA((members - 1,))],
        name="cut",
    )(place, snapshots)
    group = ("row", "col")
    received = []
    for step in range(1, members):
        pairs = [(i, i ^ step) for i in range(members)]
        received.append(lax.ppermute(cuts[step - 1], group, pairs))
    starts = [start_block] + [xor_permute(start_block, "row", mask) for mask in range(1, 4)]

    total = len(packed_blocks(tiles)) * TILE
    side = total // 2
    chunk = side // 4
    keep, send = pl.pallas_call(
        functools.partial(gram_kernel, members, shard_rows, width),
        out_shape=[jax.ShapeDtypeStruct((side, TILE), f32)] * 2,
        in_specs=[smem_spec(), any_spec()] + [any_spec()] * (members - 1),
        out_specs=[vmem_spec()] * 2,
        scratch_shapes=[
            pltpu.VMEM((snaps, width), bf16),
            pltpu.SemaphoreType.DMA((members,)),
        ],
        name="gram",
    )(place, snapshots, *received)
    got = xor_permute(send, "feat", 1)
    quarters = pl.pallas_call(
        functools.partial(quarter_kernel, chunk),
        out_shape=[jax.ShapeDtypeStruct((chunk, TILE), f32)] * 4,
        in_specs=[smem_spec(), vmem_spec(), vmem_spec()],
        out_specs=[vmem_spec()] * 4,
        name="quarter",
    )(place, keep, got)
    mine = quarters[0]
    arrived = [quad_permute(quarters[mask], mask) for mask in range(1, 4)]
    mine = (mine + arrived[0]) + (arrived[1] + arrived[2])
    others = [xor_permute(mine, "row", mask) for mask in range(1, 4)]
    mine = (mine + others[0]) + (others[1] + others[2])
    pieces = [mine] + [quad_permute(mine, mask) for mask in range(1, 4)]
    pieces = pieces + [xor_permute(piece, "feat", 1) for piece in pieces]
    return pl.pallas_call(
        functools.partial(finish_kernel, float(points), tiles, chunk, snaps),
        out_shape=jax.ShapeDtypeStruct((snaps // rows_total, vecs), f32),
        in_specs=[smem_spec()] + [any_spec()] * 12,
        out_specs=vmem_spec(),
        scratch_shapes=[
            pltpu.VMEM((total, TILE), f32),
            pltpu.VMEM((snaps, snaps), bf16),
            pltpu.VMEM((snaps, snaps), bf16),
            pltpu.VMEM((snaps, vecs), f32),
            pltpu.VMEM((vecs, snaps), f32),
            pltpu.SemaphoreType.DMA((12,)),
        ],
        name="finish",
    )(place, *pieces, *starts)


def solution(mesh):
    sizes = dict(mesh.shape)
    placed = (P(("row", "col"), "feat"), P("row", None))

    def run(snapshots, start_block):
        snaps, points = snapshots.shape
        members = sizes["row"] * sizes["col"]
        tiles = snaps // TILE
        packs = (
            sizes["row"] == 4
            and sizes["col"] == 2
            and sizes["feat"] == 4
            and snaps % (TILE * sizes["row"]) == 0
            and points % (TILE * members * sizes["feat"]) == 0
            and (tiles * (tiles + 1) // 2) % 2 == 0
            and snaps <= 1024
        )
        body = packed_body if packs else spread_body
        mapped = jax.shard_map(
            functools.partial(body, points),
            mesh=mesh,
            in_specs=placed,
            out_specs=P("row", None),
            check_vma=False,
        )
        return mapped(snapshots, start_block)

    return run
```

```python
import functools
import math

import jax
import jax.numpy as jnp
from jax import lax
from jax.experimental import pallas as pl
from jax.experimental.pallas import tpu as pltpu
from jax.sharding import PartitionSpec as P

LAGS = 128
ITERS = 6
TILE = 128


kernel_spread = 0.25
highest = lax.Precision.HIGHEST
f32 = jnp.float32
bf16 = jnp.bfloat16


def broadcast(x, axis, root):
    mine = lax.axis_index(axis) == root
    return lax.psum(jnp.where(mine, x, jnp.zeros_like(x)), axis)


def shifted(x, axis, by):
    length = lax.axis_size(axis)
    pairs = [(i, i + by) for i in range(length) if 0 <= i + by < length]
    return lax.ppermute(x, axis, pairs)


def diagonal_window(extended, lag_count):
    running = None
    offset = 0
    partial_sum = extended
    levels = lag_count.bit_length()
    for level in range(levels):
        stride = 1 << level
        if lag_count & stride:
            running = partial_sum
            offset = offset + stride
        if level + 1 < levels:
            partial_sum = partial_sum[:-stride, :-stride] + partial_sum[stride:, stride:]
    return running


def orthonormal(product, gram_sum):
    factor = jnp.linalg.cholesky(gram_sum)
    return jax.scipy.linalg.solve_triangular(factor, product.T, lower=True).T


def square_norms(fields):
    widened = fields.astype(f32)
    return jnp.sum(widened * widened, axis=1)


def spread_body(points, snapshots, start_block):
    row_total = lax.axis_size("row")
    col_total = lax.axis_size("col")
    row_place = lax.axis_index("row")
    col_place = lax.axis_index("col")
    shard_rows = snapshots.shape[0]
    block_rows = shard_rows * col_total
    pairing = row_total // col_total
    block_cols = block_rows * pairing
    own_rows = lax.all_gather(snapshots, "col", axis=0, tiled=True)
    own_norms = square_norms(own_rows)
    members = []
    for member in range(pairing):
        members.append(broadcast(own_rows, "row", pairing * col_place + member))
    col_data = jnp.concatenate(members, axis=0)
    col_norms = square_norms(col_data)
    products = lax.dot_general(
        own_rows, col_data, (((1,), (1,)), ((), ())), preferred_element_type=f32
    )
    partial_dist = own_norms[:, None] + col_norms[None, :] - 2.0 * products
    distance = lax.psum(partial_dist, "feat")
    rim_width = LAGS - 1
    top_rim = shifted(distance[block_rows - rim_width :], "row", 1)
    upper = jnp.concatenate([top_rim, distance], axis=0)
    left_side = shifted(upper[:, block_cols - rim_width :], "col", 1)
    extended = jnp.concatenate([left_side, upper], axis=1)
    lagged = diagonal_window(extended, LAGS)
    row_ids = row_place * block_rows + lax.broadcasted_iota(jnp.int32, (block_rows, block_cols), 0)
    col_ids = col_place * block_cols + lax.broadcasted_iota(jnp.int32, (block_rows, block_cols), 1)
    counts = jnp.minimum(jnp.minimum(row_ids, col_ids), rim_width) + 1
    kernel = jnp.exp(-(lagged / (counts.astype(f32) * points)) / kernel_spread)
    row_degree = lax.psum(jnp.sum(kernel, axis=1), "col")
    every_degree = lax.all_gather(row_degree, "row", axis=0, tiled=True)
    col_degree = lax.dynamic_slice_in_dim(every_degree, col_place * block_cols, block_cols)
    markov = kernel * lax.rsqrt(row_degree)[:, None] * lax.rsqrt(col_degree)[None, :]
    basis = start_block
    for rounds in range(ITERS // 2):
        product = lax.dot_general(
            markov,
            basis,
            (((0,), (0,)), ((), ())),
            precision=highest,
            preferred_element_type=f32,
        )
        summed_cols = lax.psum(product, "row")
        row_product = jnp.dot(markov, summed_cols, precision=highest, preferred_element_type=f32)
        summed_rows = lax.psum(row_product, "col")
        local_gram = jnp.dot(
            summed_rows.T, summed_rows, precision=highest, preferred_element_type=f32
        )
        gram_rows = lax.psum(local_gram, "row")
        basis = orthonormal(summed_rows, gram_rows)
    return basis * math.sqrt(row_total * block_rows)


def any_spec():
    return pl.BlockSpec(memory_space=pl.ANY)


def vmem_spec():
    return pl.BlockSpec(memory_space=pltpu.VMEM)


def near(x):
    return pltpu.with_memory_space_constraint(x, pltpu.VMEM)


def xor_permute(x, axis, mask):
    return lax.ppermute(x, axis, [(i, i ^ mask) for i in range(lax.axis_size(axis))])


def quad_permute(x, mask):
    cols, feats = lax.axis_size("col"), lax.axis_size("feat")
    pairs = []
    for col in range(cols):
        for feat in range(feats):
            there = (col ^ (mask >> 1)) * feats + (feat ^ ((mask & 1) * (feats // 2)))
            pairs.append((col * feats + feat, there))
    return lax.ppermute(x, ("col", "feat"), pairs)


def packed_blocks(tiles):
    return [(b, c) for b in range(tiles) for c in range(tiles - b)]


def device_places():
    row, col, feat = lax.axis_index("row"), lax.axis_index("col"), lax.axis_index("feat")
    return row * lax.axis_size("col") + col, feat & 1, col * 2 + (feat >> 1), row


def cut_kernel(members, width, x_ref, *refs):
    outs, sems = refs[:members], refs[members]
    me = device_places()[0]
    copies = []
    for step in range(members):
        begin = pl.multiple_of((me ^ step) * width, TILE)
        copies.append(
            pltpu.make_async_copy(x_ref.at[:, pl.ds(begin, width)], outs[step], sems.at[step])
        )
    for copy in copies:
        copy.start()
    for copy in copies:
        copy.wait()


def gram_kernel(members, rows, width, *refs):
    received, starts = refs[:members], refs[members : members + 4]
    keep_ref, send_ref, begin_ref, data_ref = refs[members + 4 :]
    me, half, _, row_place = device_places()
    for step in range(members):
        begin = pl.multiple_of((me ^ step) * rows, rows)
        data_ref[pl.ds(begin, rows), :] = received[step][...]
    span = starts[0].shape[1]
    for mask in range(4):
        begin = pl.multiple_of((row_place ^ mask) * span, TILE)
        begin_ref[:, pl.ds(begin, span)] = starts[mask][...]
    tiles = members * rows // TILE
    sub = lax.broadcasted_iota(jnp.int32, (TILE, TILE), 0)
    lane = lax.broadcasted_iota(jnp.int32, (TILE, TILE), 1)
    anti = sub + lane == TILE - 1
    flip = anti.astype(bf16)
    contract = (((1,), (1,)), ((), ()))
    strips, row_norms, col_norms = [], [], []
    for b in range(tiles):
        mirror = tiles - 1 - b
        block = data_ref[mirror * TILE : (mirror + 1) * TILE, :]
        turned = jnp.dot(flip, block, preferred_element_type=f32).astype(bf16)
        prods = lax.dot_general(
            turned, data_ref[: (mirror + 1) * TILE, :], contract, preferred_element_type=f32
        )
        strips.append(prods)
        own = jnp.where(anti, prods[:, mirror * TILE :], 0.0)
        row_norms.append(jnp.sum(own, axis=1, keepdims=True))
        col_norms.append(jnp.sum(own, axis=0, keepdims=True))
    norms = jnp.concatenate(col_norms[::-1], axis=1)
    total = len(packed_blocks(tiles))
    at = 0
    for b in range(tiles):
        span = (tiles - b) * TILE
        dist = row_norms[b] + norms[:, :span] - 2.0 * strips[b]
        turned = pltpu.roll(dist, 0, 1, stride=1, stride_axis=0)
        head = jnp.where(lane >= sub, turned[:, :TILE], 0.0)
        for c in range(tiles - b):
            value = head if c == 0 else turned[:, c * TILE : (c + 1) * TILE]
            side, slot = at // (total // 2), at % (total // 2)

            @pl.when(half == side)
            def _(value=value, slot=slot):
                keep_ref[slot * TILE : (slot + 1) * TILE, :] = value

            @pl.when(half != side)
            def _(value=value, slot=slot):
                send_ref[slot * TILE : (slot + 1) * TILE, :] = value

            at += 1


def quarter_kernel(chunk, keep_ref, got_ref, *outs):
    quad = device_places()[2]
    for mask in range(4):
        rows = pl.ds(pl.multiple_of((quad ^ mask) * chunk, 8), chunk)
        outs[mask][...] = keep_ref[rows, :] + got_ref[rows, :]


def split(x):
    high = x.astype(bf16)
    return high, (x - high.astype(f32)).astype(bf16)


def split_dot(a, b, contract=(((1,), (0,)), ((), ()))):
    a_high, a_low = split(a)
    b_high, b_low = split(b)
    rows = a.shape[0]
    stacked = jnp.concatenate([a_high, a_low], axis=0)
    first = lax.dot_general(stacked, b_high, contract, preferred_element_type=f32)
    second = lax.dot_general(a_high, b_low, contract, preferred_element_type=f32)
    return first[:rows] + (first[rows:] + second)


def inverse_factor(small):
    size = small.shape[0]
    sub = lax.broadcasted_iota(jnp.int32, (size, size), 0)
    lane = lax.broadcasted_iota(jnp.int32, (size, size), 1)
    eye = (sub == lane).astype(f32)
    work = jnp.concatenate([small, eye], axis=1)
    below = lax.broadcasted_iota(jnp.int32, (size, 1), 0)
    for k in range(size - 1):
        row = work[k : k + 1, :]
        scale = work[:, k : k + 1] / work[k : k + 1, k : k + 1]
        work = work - jnp.where(below > k, scale, 0.0) * row
    pivots = jnp.sum(work[:, :size] * eye, axis=1, keepdims=True)
    begin = jnp.sum(small * eye, axis=1, keepdims=True)
    return work[:, size:] * lax.rsqrt(pivots), jnp.min(pivots / begin)


def finish_kernel(points, tiles, chunk, snaps, *refs):
    pieces, start_ref = refs[:8], refs[8]
    out_ref, packed_ref, high_ref, low_ref, wide_ref = refs[9:]
    _, half, quad, row_place = device_places()
    for side in range(2):
        for mask in range(4):
            begin = pl.multiple_of((half ^ side) * (4 * chunk) + (quad ^ mask) * chunk, 8)
            packed_ref[pl.ds(begin, chunk), :] = pieces[side * 4 + mask][...]
    rows = snaps // 4
    sub = lax.broadcasted_iota(jnp.int32, (TILE, TILE), 0)
    lane = lax.broadcasted_iota(jnp.int32, (TILE, TILE), 1)
    late = (sub + lane >= TILE - 1).astype(bf16)
    early = (sub + lane < TILE - 1).astype(bf16)
    places = {}
    for at, (b, c) in enumerate(packed_blocks(tiles)):
        places[(b, b + c)] = at

    def strip(b, first):
        parts = []
        for c in range(first, tiles):
            at = places[(b, c)]
            parts.append(packed_ref[at * TILE : (at + 1) * TILE, :])
        whole = jnp.concatenate(parts, axis=1) if len(parts) > 1 else parts[0]
        high = whole.astype(bf16)
        rest = whole - high.astype(f32)
        middle = rest.astype(bf16)
        low = (rest - middle.astype(f32)).astype(bf16)
        return high, middle, low

    strips = [strip(b, b) for b in range(tiles)]
    for block in range(tiles):
        b = tiles - 1 - block
        span = (block + 1) * TILE
        lagged = None
        for piece in strips[b]:
            term = jnp.dot(late, piece, preferred_element_type=f32)
            lagged = term if lagged is None else lagged + term
        if block > 0:
            more = None
            for piece in strips[b + 1]:
                term = jnp.dot(early, piece, preferred_element_type=f32)
                more = term if more is None else more + term
            lagged = jnp.concatenate([lagged[:, :TILE], lagged[:, TILE:] + more], axis=1)
        lagged = pltpu.roll(lagged, (1 + span - TILE) % span, 1, stride=1, stride_axis=0)
        columns = lax.broadcasted_iota(jnp.int32, (1, span), 1)
        counts = (jnp.minimum(columns, LAGS - 1) + 1).astype(f32)
        kernel = jnp.exp(lagged * (-1.0 / (counts * (points * kernel_spread))))
        for c in range(block + 1):
            value = kernel[:, c * TILE : (c + 1) * TILE]
            if c == block:
                value = jnp.where(lane <= sub, value, value.T)
            high, low = split(value)
            high_ref[block * TILE : (block + 1) * TILE, c * TILE : (c + 1) * TILE] = high
            low_ref[block * TILE : (block + 1) * TILE, c * TILE : (c + 1) * TILE] = low
            if c < block:
                high, low = split(value.T)
                high_ref[c * TILE : (c + 1) * TILE, block * TILE : (block + 1) * TILE] = high
                low_ref[c * TILE : (c + 1) * TILE, block * TILE : (block + 1) * TILE] = low
    ones = jnp.ones((16, snaps), bf16)
    degrees = jnp.dot(ones, high_ref[...], preferred_element_type=f32)
    degrees = degrees + jnp.dot(ones, low_ref[...], preferred_element_type=f32)
    inverse = 1.0 / degrees[0:1, :]
    scales = lax.sqrt(inverse)
    vecs = start_ref.shape[0]
    start = start_ref[...]

    def apply(x):
        x_high, x_low = split(x)
        stacked = jnp.concatenate([x_high, x_low], axis=0)
        first = jnp.dot(stacked, high_ref[...], preferred_element_type=f32)
        second = jnp.dot(x_high, low_ref[...], preferred_element_type=f32)
        return first[:vecs] + (first[vecs:] + second)

    across = (((1,), (1,)), ((), ()))

    def rounds(x, least, times):
        x = apply(x * scales)
        for _ in range(times - 1):
            x = apply(x * inverse)
        x = x * scales
        factor, ratio = inverse_factor(split_dot(x, x, across))
        return split_dot(factor, x), jnp.minimum(least, ratio)

    def loop(times):
        return lax.fori_loop(
            0, ITERS // times, lambda _, c: rounds(c[0], c[1], times), (start, f32(1.0))
        )

    basis, least = loop(3)
    wide_ref[...] = basis

    @pl.when(jnp.logical_not(least > 1e-4))
    def _():
        wide_ref[...] = loop(1)[0]

    basis = wide_ref[...]
    eye_sub = lax.broadcasted_iota(jnp.int32, (vecs, vecs), 0)
    eye_lane = lax.broadcasted_iota(jnp.int32, (vecs, vecs), 1)
    error = split_dot(basis, basis, across) - (eye_sub == eye_lane).astype(f32)
    weight = jnp.where(eye_sub > eye_lane, 1.0, jnp.where(eye_sub == eye_lane, 0.5, 0.0))
    wide_ref[...] = (basis - split_dot(error * weight, basis)) * math.sqrt(snaps)
    out_ref[...] = wide_ref[:, pl.ds(pl.multiple_of(row_place * rows, TILE), rows)]


def packed_body(points, snapshots, start_block):
    cols, feats = lax.axis_size("col"), lax.axis_size("feat")
    rows_total = lax.axis_size("row")
    members = rows_total * cols
    shard_rows, shard_points = snapshots.shape
    width = shard_points // members
    snaps = shard_rows * members
    tiles = snaps // TILE
    vecs = start_block.shape[1]
    cuts = pl.pallas_call(
        functools.partial(cut_kernel, members, width),
        out_shape=[pltpu.VMEM((shard_rows, width), bf16)] * members,
        in_specs=[any_spec()],
        out_specs=[vmem_spec()] * members,
        scratch_shapes=[pltpu.SemaphoreType.DMA((members,))],
        name="cut",
    )(snapshots)
    received = [cuts[0]] + [None] * (members - 1)
    for step in (4, 6, 5, 7, 2, 3, 1):
        pairs = [(i, i ^ step) for i in range(members)]
        received[step] = lax.ppermute(cuts[step], ("row", "col"), pairs)
    turned = start_block.T
    starts = [turned] + [xor_permute(turned, "row", mask) for mask in range(1, 4)]

    total = len(packed_blocks(tiles)) * TILE
    side = total // 2
    chunk = side // 4
    keep, send, begin = pl.pallas_call(
        functools.partial(gram_kernel, members, shard_rows, width),
        out_shape=[pltpu.VMEM((side, TILE), f32)] * 2 + [pltpu.VMEM((vecs, snaps), f32)],
        in_specs=[vmem_spec()] * (members + 4),
        out_specs=[vmem_spec()] * 3,
        scratch_shapes=[pltpu.VMEM((snaps, width), bf16)],
        name="gram",
    )(*[near(x) for x in received + starts])
    got = xor_permute(send, "feat", 1)
    quarters = pl.pallas_call(
        functools.partial(quarter_kernel, chunk),
        out_shape=[pltpu.VMEM((chunk, TILE), f32)] * 4,
        in_specs=[vmem_spec()] * 2,
        out_specs=[vmem_spec()] * 4,
        name="quarter",
    )(near(keep), near(got))
    mine = quarters[0]
    arrived = [quad_permute(quarters[mask], mask) for mask in range(1, 4)]
    mine = (mine + arrived[0]) + (arrived[1] + arrived[2])
    others = [xor_permute(mine, "row", mask) for mask in range(1, 4)]
    mine = (mine + others[0]) + (others[1] + others[2])
    pieces = [mine] + [quad_permute(mine, mask) for mask in range(1, 4)]
    pieces = pieces + [xor_permute(piece, "feat", 1) for piece in pieces]
    basis = pl.pallas_call(
        functools.partial(finish_kernel, float(points), tiles, chunk, snaps),
        out_shape=jax.ShapeDtypeStruct((vecs, snaps // rows_total), f32),
        in_specs=[vmem_spec()] * 9,
        out_specs=vmem_spec(),
        scratch_shapes=[
            pltpu.VMEM((total, TILE), f32),
            pltpu.VMEM((snaps, snaps), bf16),
            pltpu.VMEM((snaps, snaps), bf16),
            pltpu.VMEM((vecs, snaps), f32),
        ],
        name="finish",
    )(*[near(x) for x in pieces + [begin]])
    return basis.T


def solution(mesh):
    sizes = dict(mesh.shape)
    placed = (P(("row", "col"), "feat"), P("row", None))

    def run(snapshots, start_block):
        snaps, points = snapshots.shape
        members = sizes["row"] * sizes["col"]
        tiles = snaps // TILE
        packs = (
            sizes["row"] == 4
            and sizes["col"] == 2
            and sizes["feat"] == 4
            and snaps % (TILE * sizes["row"]) == 0
            and points % (TILE * members * sizes["feat"]) == 0
            and (tiles * (tiles + 1) // 2) % 2 == 0
            and snaps <= 1024
        )
        body = packed_body if packs else spread_body
        mapped = jax.shard_map(
            functools.partial(body, points),
            mesh=mesh,
            in_specs=placed,
            out_specs=P("row", None),
            check_vma=False,
        )
        return mapped(snapshots, start_block)

    return run
```

```python
import functools
import math

import jax
import jax.numpy as jnp
from jax import lax
from jax.experimental import pallas as pl
from jax.experimental.pallas import tpu as pltpu
from jax.sharding import PartitionSpec as P

LAGS = 128
ITERS = 6
TILE = 128
PANEL = 16


kernel_spread = 0.25
highest = lax.Precision.HIGHEST
f32 = jnp.float32
bf16 = jnp.bfloat16


def broadcast(x, axis, root):
    mine = lax.axis_index(axis) == root
    return lax.psum(jnp.where(mine, x, jnp.zeros_like(x)), axis)


def shifted(x, axis, by):
    length = lax.axis_size(axis)
    pairs = [(i, i + by) for i in range(length) if 0 <= i + by < length]
    return lax.ppermute(x, axis, pairs)


def diagonal_window(extended, lag_count):
    running = None
    offset = 0
    partial_sum = extended
    levels = lag_count.bit_length()
    for level in range(levels):
        stride = 1 << level
        if lag_count & stride:
            running = partial_sum
            offset = offset + stride
        if level + 1 < levels:
            partial_sum = partial_sum[:-stride, :-stride] + partial_sum[stride:, stride:]
    return running


def orthonormal(product, gram_sum):
    factor = jnp.linalg.cholesky(gram_sum)
    return jax.scipy.linalg.solve_triangular(factor, product.T, lower=True).T


def square_norms(fields):
    widened = fields.astype(f32)
    return jnp.sum(widened * widened, axis=1)


def spread_body(points, snapshots, start_block):
    row_total = lax.axis_size("row")
    col_total = lax.axis_size("col")
    row_place = lax.axis_index("row")
    col_place = lax.axis_index("col")
    shard_rows = snapshots.shape[0]
    block_rows = shard_rows * col_total
    pairing = row_total // col_total
    block_cols = block_rows * pairing
    own_rows = lax.all_gather(snapshots, "col", axis=0, tiled=True)
    own_norms = square_norms(own_rows)
    members = []
    for member in range(pairing):
        members.append(broadcast(own_rows, "row", pairing * col_place + member))
    col_data = jnp.concatenate(members, axis=0)
    col_norms = square_norms(col_data)
    products = lax.dot_general(
        own_rows, col_data, (((1,), (1,)), ((), ())), preferred_element_type=f32
    )
    partial_dist = own_norms[:, None] + col_norms[None, :] - 2.0 * products
    distance = lax.psum(partial_dist, "feat")
    rim_width = LAGS - 1
    top_rim = shifted(distance[block_rows - rim_width :], "row", 1)
    upper = jnp.concatenate([top_rim, distance], axis=0)
    left_side = shifted(upper[:, block_cols - rim_width :], "col", 1)
    extended = jnp.concatenate([left_side, upper], axis=1)
    lagged = diagonal_window(extended, LAGS)
    row_ids = row_place * block_rows + lax.broadcasted_iota(jnp.int32, (block_rows, block_cols), 0)
    col_ids = col_place * block_cols + lax.broadcasted_iota(jnp.int32, (block_rows, block_cols), 1)
    counts = jnp.minimum(jnp.minimum(row_ids, col_ids), rim_width) + 1
    kernel = jnp.exp(-(lagged / (counts.astype(f32) * points)) / kernel_spread)
    row_degree = lax.psum(jnp.sum(kernel, axis=1), "col")
    every_degree = lax.all_gather(row_degree, "row", axis=0, tiled=True)
    col_degree = lax.dynamic_slice_in_dim(every_degree, col_place * block_cols, block_cols)
    markov = kernel * lax.rsqrt(row_degree)[:, None] * lax.rsqrt(col_degree)[None, :]
    basis = start_block
    for rounds in range(ITERS // 2):
        product = lax.dot_general(
            markov,
            basis,
            (((0,), (0,)), ((), ())),
            precision=highest,
            preferred_element_type=f32,
        )
        summed_cols = lax.psum(product, "row")
        row_product = jnp.dot(markov, summed_cols, precision=highest, preferred_element_type=f32)
        summed_rows = lax.psum(row_product, "col")
        local_gram = jnp.dot(
            summed_rows.T, summed_rows, precision=highest, preferred_element_type=f32
        )
        gram_rows = lax.psum(local_gram, "row")
        basis = orthonormal(summed_rows, gram_rows)
    return basis * math.sqrt(row_total * block_rows)


def any_spec():
    return pl.BlockSpec(memory_space=pl.ANY)


def vmem_spec():
    return pl.BlockSpec(memory_space=pltpu.VMEM)


def near(x):
    return pltpu.with_memory_space_constraint(x, pltpu.VMEM)


def xor_permute(x, axis, mask):
    return lax.ppermute(x, axis, [(i, i ^ mask) for i in range(lax.axis_size(axis))])


def quad_permute(x, mask):
    cols, feats = lax.axis_size("col"), lax.axis_size("feat")
    pairs = []
    for col in range(cols):
        for feat in range(feats):
            there = (col ^ (mask >> 1)) * feats + (feat ^ ((mask & 1) * (feats // 2)))
            pairs.append((col * feats + feat, there))
    return lax.ppermute(x, ("col", "feat"), pairs)


def packed_blocks(tiles):
    full = [(b, c) for b in range(tiles) for c in range(tiles - 1 - b)]
    return full, [(b, b + 1) for b in range(0, tiles, 2)]


def ring_steps(rows, cols):
    shifts = [rows // 2, 1, rows - 1]
    steps = [(a, (n + turn) % cols) for turn in range(cols) for n, a in enumerate(shifts)]
    return [(0, 0)] + steps + [(0, mask) for mask in range(1, cols)]


def device_places():
    row, col, feat = lax.axis_index("row"), lax.axis_index("col"), lax.axis_index("feat")
    return feat & 1, col * 2 + (feat >> 1), row, col


def cut_kernel(steps, rows_total, cols, width, x_ref, *refs):
    members = len(steps)
    outs, sems = refs[:members], refs[members]
    _, _, row, col = device_places()
    copies = []
    for step, (shift, mask) in enumerate(steps):
        there = lax.rem(row + shift, rows_total) * cols + (col ^ mask)
        begin = pl.multiple_of(there * width, TILE)
        copies.append(
            pltpu.make_async_copy(x_ref.at[:, pl.ds(begin, width)], outs[step], sems.at[step])
        )
    for copy in copies:
        copy.start()
    for copy in copies:
        copy.wait()


def gram_kernel(steps, rows_total, cols, rows, *refs):
    members = len(steps)
    received, starts = refs[:members], refs[members : members + 4]
    keep_ref, send_ref, begin_ref, data_ref = refs[members + 4 :]
    half, _, row_place, col_place = device_places()
    for step, (shift, mask) in enumerate(steps):
        source = lax.rem(row_place + (rows_total - shift), rows_total) * cols + (col_place ^ mask)
        data_ref[pl.ds(pl.multiple_of(source * rows, rows), rows), :] = received[step][...]
    span = starts[0].shape[1]
    for mask in range(4):
        begin = pl.multiple_of((row_place ^ mask) * span, TILE)
        begin_ref[:, pl.ds(begin, span)] = starts[mask][...]
    tiles = members * rows // TILE
    sub = lax.broadcasted_iota(jnp.int32, (TILE, TILE), 0)
    lane = lax.broadcasted_iota(jnp.int32, (TILE, TILE), 1)
    anti = sub + lane == TILE - 1
    flip = anti.astype(bf16)
    contract = (((1,), (1,)), ((), ()))
    strips, row_norms, col_norms = [], [], []
    for b in range(tiles):
        mirror = tiles - 1 - b
        block = data_ref[mirror * TILE : (mirror + 1) * TILE, :]
        turned = jnp.dot(flip, block, preferred_element_type=f32).astype(bf16)
        prods = lax.dot_general(
            turned, data_ref[: (mirror + 1) * TILE, :], contract, preferred_element_type=f32
        )
        strips.append(prods)
        own = jnp.where(anti, prods[:, mirror * TILE :], 0.0)
        row_norms.append(jnp.sum(own, axis=1, keepdims=True))
        col_norms.append(jnp.sum(own, axis=0, keepdims=True))
    norms = jnp.concatenate(col_norms[::-1], axis=1)
    dists = []
    for b in range(tiles):
        span = (tiles - b) * TILE
        dists.append(row_norms[b] + norms[:, :span] - 2.0 * strips[b])
    full, pairs = packed_blocks(tiles)
    values = [dists[b][:, c * TILE : (c + 1) * TILE] for b, c in full]
    for one, two in pairs:
        first = dists[one][:, -TILE:]
        second = dists[two][:, -TILE:]
        values.append(jnp.where(sub + lane < TILE - 1, first, second))
    for at, value in enumerate(values):
        side, slot = at // (len(values) // 2), at % (len(values) // 2)

        @pl.when(half == side)
        def _(value=value, slot=slot):
            keep_ref[slot * TILE : (slot + 1) * TILE, :] = value

        @pl.when(half != side)
        def _(value=value, slot=slot):
            send_ref[slot * TILE : (slot + 1) * TILE, :] = value


def quarter_kernel(chunk, keep_ref, got_ref, *outs):
    quad = device_places()[1]
    for mask in range(4):
        rows = pl.ds(pl.multiple_of((quad ^ mask) * chunk, 8), chunk)
        outs[mask][...] = keep_ref[rows, :] + got_ref[rows, :]


def split(x):
    high = x.astype(bf16)
    return high, (x - high.astype(f32)).astype(bf16)


def split_dot(a, b, contract=(((1,), (0,)), ((), ()))):
    a_high, a_low = split(a)
    b_high, b_low = split(b)
    rows = a.shape[0]
    stacked = jnp.concatenate([a_high, a_low], axis=0)
    first = lax.dot_general(stacked, b_high, contract, preferred_element_type=f32)
    second = lax.dot_general(a_high, b_low, contract, preferred_element_type=f32)
    return first[:rows] + (first[rows:] + second)


def inverse_factor(small):
    size = small.shape[0]
    sub = lax.broadcasted_iota(jnp.int32, (size, size), 0)
    lane = lax.broadcasted_iota(jnp.int32, (size, size), 1)
    eye = (sub == lane).astype(f32)
    work = jnp.concatenate([small, eye], axis=1)
    wide = work.shape
    below = lax.broadcasted_iota(jnp.int32, wide, 0)
    for first in range(0, size, PANEL):
        columns = [
            jnp.broadcast_to(work[:, first + a : first + a + 1], wide) for a in range(PANEL)
        ]
        for a in range(PANEL):
            k = first + a
            if k == size - 1:
                break
            scale = columns[a] / columns[a][k : k + 1, :]
            scale = jnp.where(below > k, scale, 0.0)
            for b in range(a + 1, PANEL):
                columns[b] = columns[b] - scale * columns[b][k : k + 1, :]
            work = work - scale * work[k : k + 1, :]
    pivots = jnp.sum(work[:, :size] * eye, axis=1, keepdims=True)
    begin = jnp.sum(small * eye, axis=1, keepdims=True)
    return work[:, size:] * lax.rsqrt(pivots), jnp.min(pivots / begin)


def finish_kernel(points, tiles, chunk, snaps, *refs):
    pieces, start_ref = refs[:8], refs[8]
    out_ref, packed_ref, high_ref, low_ref, wide_ref = refs[9:]
    half, quad, row_place, _ = device_places()
    for side in range(2):
        for mask in range(4):
            begin = pl.multiple_of((half ^ side) * (4 * chunk) + (quad ^ mask) * chunk, 8)
            packed_ref[pl.ds(begin, chunk), :] = pieces[side * 4 + mask][...]
    rows = snaps // 4
    sub = lax.broadcasted_iota(jnp.int32, (TILE, TILE), 0)
    lane = lax.broadcasted_iota(jnp.int32, (TILE, TILE), 1)
    late = (sub + lane >= TILE - 1).astype(bf16)
    early = (sub + lane < TILE - 1).astype(bf16)
    flip = (sub + lane == TILE - 1).astype(bf16)
    full, pairs = packed_blocks(tiles)

    def block_at(at):
        return packed_ref[at * TILE : (at + 1) * TILE, :]

    def pieces_of(whole):
        high = whole.astype(bf16)
        rest = whole - high.astype(f32)
        middle = rest.astype(bf16)
        return high, middle, (rest - middle.astype(f32)).astype(bf16)

    def mirrored(value):
        total = None
        for piece in pieces_of(value):
            turned = lax.dot_general(
                flip, piece, (((1,), (1,)), ((), ())), preferred_element_type=f32
            )
            term = jnp.dot(turned.astype(bf16), flip, preferred_element_type=f32)
            total = term if total is None else total + term
        return total

    corners = {}
    for at, (one, two) in enumerate(pairs):
        shared = block_at(len(full) + at)
        corners[one] = jnp.where(sub + lane < TILE - 1, shared, 0.0)
        corners[two] = mirrored(jnp.where(sub + lane > TILE - 1, shared, 0.0))

    def strip(b):
        parts = [block_at(at) for at, place in enumerate(full) if place[0] == b]
        whole = jnp.concatenate(parts + [corners[b]], axis=1) if parts else corners[b]
        return pieces_of(pltpu.roll(whole, 0, 1, stride=1, stride_axis=0))

    strips = [strip(b) for b in range(tiles)]
    for block in range(tiles):
        b = tiles - 1 - block
        span = (block + 1) * TILE
        lagged = None
        for piece in strips[b]:
            term = jnp.dot(late, piece, preferred_element_type=f32)
            lagged = term if lagged is None else lagged + term
        if block > 0:
            more = None
            for piece in strips[b + 1]:
                term = jnp.dot(early, piece, preferred_element_type=f32)
                more = term if more is None else more + term
            lagged = jnp.concatenate([lagged[:, :TILE], lagged[:, TILE:] + more], axis=1)
        lagged = pltpu.roll(lagged, (1 + span - TILE) % span, 1, stride=1, stride_axis=0)
        columns = lax.broadcasted_iota(jnp.int32, (1, span), 1)
        counts = (jnp.minimum(columns, LAGS - 1) + 1).astype(f32)
        kernel = jnp.exp(lagged * (-1.0 / (counts * (points * kernel_spread))))
        for c in range(block + 1):
            value = kernel[:, c * TILE : (c + 1) * TILE]
            if c == block:
                value = jnp.where(lane <= sub, value, value.T)
            high, low = split(value)
            high_ref[block * TILE : (block + 1) * TILE, c * TILE : (c + 1) * TILE] = high
            low_ref[block * TILE : (block + 1) * TILE, c * TILE : (c + 1) * TILE] = low
            if c < block:
                high, low = split(value.T)
                high_ref[c * TILE : (c + 1) * TILE, block * TILE : (block + 1) * TILE] = high
                low_ref[c * TILE : (c + 1) * TILE, block * TILE : (block + 1) * TILE] = low
    ones = jnp.ones((16, snaps), bf16)
    degrees = jnp.dot(ones, high_ref[...], preferred_element_type=f32)
    degrees = degrees + jnp.dot(ones, low_ref[...], preferred_element_type=f32)
    inverse = 1.0 / degrees[0:1, :]
    scales = lax.sqrt(inverse)
    vecs = start_ref.shape[0]
    start = start_ref[...]

    def apply(x):
        x_high, x_low = split(x)
        stacked = jnp.concatenate([x_high, x_low], axis=0)
        first = jnp.dot(stacked, high_ref[...], preferred_element_type=f32)
        second = jnp.dot(x_high, low_ref[...], preferred_element_type=f32)
        return first[:vecs] + (first[vecs:] + second)

    across = (((1,), (1,)), ((), ()))

    def rounds(x, least, times):
        x = apply(x * scales)
        for _ in range(times - 1):
            x = apply(x * inverse)
        x = x * scales
        factor, ratio = inverse_factor(split_dot(x, x, across))
        return split_dot(factor, x), jnp.minimum(least, ratio)

    def loop(times):
        return lax.fori_loop(
            0,
            ITERS // times,
            lambda _, c: rounds(c[0], c[1], times),
            (start, f32(1.0)),
            unroll=times == 3,
        )

    basis, least = loop(3)
    wide_ref[...] = basis

    @pl.when(jnp.logical_not(least > 1e-4))
    def _():
        wide_ref[...] = loop(1)[0]

    basis = wide_ref[...]
    eye_sub = lax.broadcasted_iota(jnp.int32, (vecs, vecs), 0)
    eye_lane = lax.broadcasted_iota(jnp.int32, (vecs, vecs), 1)
    error = split_dot(basis, basis, across) - (eye_sub == eye_lane).astype(f32)
    weight = jnp.where(eye_sub > eye_lane, 1.0, jnp.where(eye_sub == eye_lane, 0.5, 0.0))
    wide_ref[...] = (basis - split_dot(error * weight, basis)) * math.sqrt(snaps)
    out_ref[...] = wide_ref[:, pl.ds(pl.multiple_of(row_place * rows, TILE), rows)]


def packed_body(points, snapshots, start_block):
    cols, feats = lax.axis_size("col"), lax.axis_size("feat")
    rows_total = lax.axis_size("row")
    members = rows_total * cols
    shard_rows, shard_points = snapshots.shape
    width = shard_points // members
    snaps = shard_rows * members
    tiles = snaps // TILE
    vecs = start_block.shape[1]
    steps = ring_steps(rows_total, cols)
    cuts = pl.pallas_call(
        functools.partial(cut_kernel, steps, rows_total, cols, width),
        out_shape=[pltpu.VMEM((shard_rows, width), bf16)] * members,
        in_specs=[any_spec()],
        out_specs=[vmem_spec()] * members,
        scratch_shapes=[pltpu.SemaphoreType.DMA((members,))],
        name="cut",
    )(snapshots)
    received = [cuts[0]]
    for cut, (shift, mask) in zip(cuts[1:], steps[1:]):
        pairs = []
        for row in range(rows_total):
            for col in range(cols):
                there = (row + shift) % rows_total * cols + (col ^ mask)
                pairs.append((row * cols + col, there))
        received.append(lax.ppermute(cut, ("row", "col"), pairs))
    turned = start_block.T
    starts = [turned] + [xor_permute(turned, "row", mask) for mask in range(1, 4)]

    full, shared = packed_blocks(tiles)
    total = (len(full) + len(shared)) * TILE
    side = total // 2
    chunk = side // 4
    keep, send, begin = pl.pallas_call(
        functools.partial(gram_kernel, steps, rows_total, cols, shard_rows),
        out_shape=[pltpu.VMEM((side, TILE), f32)] * 2 + [pltpu.VMEM((vecs, snaps), f32)],
        in_specs=[vmem_spec()] * (members + 4),
        out_specs=[vmem_spec()] * 3,
        scratch_shapes=[pltpu.VMEM((snaps, width), bf16)],
        name="gram",
    )(*[near(x) for x in received + starts])
    got = xor_permute(send, "feat", 1)
    quarters = pl.pallas_call(
        functools.partial(quarter_kernel, chunk),
        out_shape=[pltpu.VMEM((chunk, TILE), f32)] * 4,
        in_specs=[vmem_spec()] * 2,
        out_specs=[vmem_spec()] * 4,
        name="quarter",
    )(near(keep), near(got))
    mine = quarters[0]
    arrived = {mask: quad_permute(quarters[mask], mask) for mask in (3, 1, 2)}
    mine = (mine + arrived[1]) + (arrived[2] + arrived[3])
    others = {mask: xor_permute(mine, "row", mask) for mask in (1, 2, 3)}
    mine = (mine + others[1]) + (others[2] + others[3])
    pieces = [mine] + [quad_permute(mine, mask) for mask in range(1, 4)]
    pieces = pieces + [xor_permute(piece, "feat", 1) for piece in pieces]
    basis = pl.pallas_call(
        functools.partial(finish_kernel, float(points), tiles, chunk, snaps),
        out_shape=jax.ShapeDtypeStruct((vecs, snaps // rows_total), f32),
        in_specs=[vmem_spec()] * 9,
        out_specs=vmem_spec(),
        scratch_shapes=[
            pltpu.VMEM((total, TILE), f32),
            pltpu.VMEM((snaps, snaps), bf16),
            pltpu.VMEM((snaps, snaps), bf16),
            pltpu.VMEM((vecs, snaps), f32),
        ],
        name="finish",
    )(*[near(x) for x in pieces + [begin]])
    return basis.T


def solution(mesh):
    sizes = dict(mesh.shape)
    placed = (P(("row", "col"), "feat"), P("row", None))

    def run(snapshots, start_block):
        snaps, points = snapshots.shape
        members = sizes["row"] * sizes["col"]
        tiles = snaps // TILE
        packs = (
            sizes["row"] == 4
            and sizes["col"] == 2
            and sizes["feat"] == 4
            and snaps % (TILE * sizes["row"]) == 0
            and points % (TILE * members * sizes["feat"]) == 0
            and (tiles * tiles // 2) % 2 == 0
            and snaps <= 1024
        )
        body = packed_body if packs else spread_body
        mapped = jax.shard_map(
            functools.partial(body, points),
            mesh=mesh,
            in_specs=placed,
            out_specs=P("row", None),
            check_vma=False,
        )
        return mapped(snapshots, start_block)

    return run
```

```python
import functools
import math

import jax
import jax.numpy as jnp
from jax import lax
from jax.experimental import pallas as pl
from jax.experimental.pallas import tpu as pltpu
from jax.sharding import PartitionSpec as P

LAGS = 128
ITERS = 6
TILE = 128
PANEL = 16


kernel_spread = 0.25
highest = lax.Precision.HIGHEST
f32 = jnp.float32
bf16 = jnp.bfloat16


def broadcast(x, axis, root):
    mine = lax.axis_index(axis) == root
    return lax.psum(jnp.where(mine, x, jnp.zeros_like(x)), axis)


def shifted(x, axis, by):
    length = lax.axis_size(axis)
    pairs = [(i, i + by) for i in range(length) if 0 <= i + by < length]
    return lax.ppermute(x, axis, pairs)


def diagonal_window(extended, lag_count):
    running = None
    offset = 0
    partial_sum = extended
    levels = lag_count.bit_length()
    for level in range(levels):
        stride = 1 << level
        if lag_count & stride:
            running = partial_sum
            offset = offset + stride
        if level + 1 < levels:
            partial_sum = partial_sum[:-stride, :-stride] + partial_sum[stride:, stride:]
    return running


def orthonormal(product, gram_sum):
    factor = jnp.linalg.cholesky(gram_sum)
    return jax.scipy.linalg.solve_triangular(factor, product.T, lower=True).T


def square_norms(fields):
    widened = fields.astype(f32)
    return jnp.sum(widened * widened, axis=1)


def spread_body(points, snapshots, start_block):
    row_total = lax.axis_size("row")
    col_total = lax.axis_size("col")
    row_place = lax.axis_index("row")
    col_place = lax.axis_index("col")
    shard_rows = snapshots.shape[0]
    block_rows = shard_rows * col_total
    pairing = row_total // col_total
    block_cols = block_rows * pairing
    own_rows = lax.all_gather(snapshots, "col", axis=0, tiled=True)
    own_norms = square_norms(own_rows)
    members = []
    for member in range(pairing):
        members.append(broadcast(own_rows, "row", pairing * col_place + member))
    col_data = jnp.concatenate(members, axis=0)
    col_norms = square_norms(col_data)
    products = lax.dot_general(
        own_rows, col_data, (((1,), (1,)), ((), ())), preferred_element_type=f32
    )
    partial_dist = own_norms[:, None] + col_norms[None, :] - 2.0 * products
    distance = lax.psum(partial_dist, "feat")
    rim_width = LAGS - 1
    top_rim = shifted(distance[block_rows - rim_width :], "row", 1)
    upper = jnp.concatenate([top_rim, distance], axis=0)
    left_side = shifted(upper[:, block_cols - rim_width :], "col", 1)
    extended = jnp.concatenate([left_side, upper], axis=1)
    lagged = diagonal_window(extended, LAGS)
    row_ids = row_place * block_rows + lax.broadcasted_iota(jnp.int32, (block_rows, block_cols), 0)
    col_ids = col_place * block_cols + lax.broadcasted_iota(jnp.int32, (block_rows, block_cols), 1)
    counts = jnp.minimum(jnp.minimum(row_ids, col_ids), rim_width) + 1
    kernel = jnp.exp(-(lagged / (counts.astype(f32) * points)) / kernel_spread)
    row_degree = lax.psum(jnp.sum(kernel, axis=1), "col")
    every_degree = lax.all_gather(row_degree, "row", axis=0, tiled=True)
    col_degree = lax.dynamic_slice_in_dim(every_degree, col_place * block_cols, block_cols)
    markov = kernel * lax.rsqrt(row_degree)[:, None] * lax.rsqrt(col_degree)[None, :]
    basis = start_block
    for rounds in range(ITERS // 2):
        product = lax.dot_general(
            markov,
            basis,
            (((0,), (0,)), ((), ())),
            precision=highest,
            preferred_element_type=f32,
        )
        summed_cols = lax.psum(product, "row")
        row_product = jnp.dot(markov, summed_cols, precision=highest, preferred_element_type=f32)
        summed_rows = lax.psum(row_product, "col")
        local_gram = jnp.dot(
            summed_rows.T, summed_rows, precision=highest, preferred_element_type=f32
        )
        gram_rows = lax.psum(local_gram, "row")
        basis = orthonormal(summed_rows, gram_rows)
    return basis * math.sqrt(row_total * block_rows)


def any_spec():
    return pl.BlockSpec(memory_space=pl.ANY)


def vmem_spec():
    return pl.BlockSpec(memory_space=pltpu.VMEM)


def near(x):
    return pltpu.with_memory_space_constraint(x, pltpu.VMEM)


def xor_permute(x, axis, mask):
    return lax.ppermute(x, axis, [(i, i ^ mask) for i in range(lax.axis_size(axis))])


def quad_permute(x, mask):
    cols, feats = lax.axis_size("col"), lax.axis_size("feat")
    pairs = []
    for col in range(cols):
        for feat in range(feats):
            there = (col ^ (mask >> 1)) * feats + (feat ^ ((mask & 1) * (feats // 2)))
            pairs.append((col * feats + feat, there))
    return lax.ppermute(x, ("col", "feat"), pairs)


def packed_blocks(tiles):
    full = [(b, c) for b in range(tiles) for c in range(b)]
    return full, [(b, b + 1) for b in range(0, tiles, 2)]


def ring_steps(rows, cols):
    shifts = [rows // 2, 1, rows - 1]
    steps = [(a, (n + turn) % cols) for turn in range(cols) for n, a in enumerate(shifts)]
    return [(0, 0)] + steps + [(0, mask) for mask in range(1, cols)]


def device_places():
    row, col, feat = lax.axis_index("row"), lax.axis_index("col"), lax.axis_index("feat")
    return feat & 1, col * 2 + (feat >> 1), row, col


def cut_kernel(steps, rows_total, cols, width, x_ref, *refs):
    members = len(steps)
    outs, sems = refs[:members], refs[members]
    _, _, row, col = device_places()
    copies = []
    for step, (shift, mask) in enumerate(steps):
        there = lax.rem(row + shift, rows_total) * cols + (col ^ mask)
        begin = pl.multiple_of(there * width, TILE)
        copies.append(
            pltpu.make_async_copy(x_ref.at[:, pl.ds(begin, width)], outs[step], sems.at[step])
        )
    for copy in copies:
        copy.start()
    for copy in copies:
        copy.wait()


def pieces_of(whole):
    high = whole.astype(bf16)
    rest = whole - high.astype(f32)
    middle = rest.astype(bf16)
    return high, middle, (rest - middle.astype(f32)).astype(bf16)


def add_dots(weights, pieces):
    total = None
    for piece in pieces:
        term = jnp.dot(weights, piece, preferred_element_type=f32)
        total = term if total is None else total + term
    return total


def gram_kernel(steps, rows_total, cols, rows, *refs):
    members = len(steps)
    received, starts = refs[:members], refs[members : members + 4]
    keep_ref, send_ref, begin_ref, data_ref = refs[members + 4 :]
    half, _, row_place, col_place = device_places()
    for step, (shift, mask) in enumerate(steps):
        source = lax.rem(row_place + (rows_total - shift), rows_total) * cols + (col_place ^ mask)
        data_ref[pl.ds(pl.multiple_of(source * rows, rows), rows), :] = received[step][...]
    span = starts[0].shape[1]
    for mask in range(4):
        begin = pl.multiple_of((row_place ^ mask) * span, TILE)
        begin_ref[:, pl.ds(begin, span)] = starts[mask][...]
    tiles = members * rows // TILE
    sub = lax.broadcasted_iota(jnp.int32, (TILE, TILE), 0)
    lane = lax.broadcasted_iota(jnp.int32, (TILE, TILE), 1)
    anti = sub + lane == TILE - 1
    flip = anti.astype(bf16)
    contract = (((1,), (1,)), ((), ()))
    strips, row_norms, col_norms = [], [], []
    for b in range(tiles):
        mirror = tiles - 1 - b
        block = data_ref[mirror * TILE : (mirror + 1) * TILE, :]
        turned = jnp.dot(flip, block, preferred_element_type=f32).astype(bf16)
        prods = lax.dot_general(
            turned, data_ref[: (mirror + 1) * TILE, :], contract, preferred_element_type=f32
        )
        strips.append(prods)
        own = jnp.where(anti, prods[:, mirror * TILE :], 0.0)
        row_norms.append(jnp.sum(own, axis=1, keepdims=True))
        col_norms.append(jnp.sum(own, axis=0, keepdims=True))
    norms = jnp.concatenate(col_norms[::-1], axis=1)
    late = (sub + lane >= TILE - 1).astype(bf16)
    early = (sub + lane < TILE - 1).astype(bf16)
    skewed = []
    for b in range(tiles):
        span = (tiles - b) * TILE
        dist = row_norms[b] + norms[:, :span] - 2.0 * strips[b]
        dist = pltpu.roll(dist, 0, 1, stride=1, stride_axis=0)
        head = jnp.where(lane >= sub, dist[:, :TILE], 0.0)
        if span > TILE:
            head = jnp.concatenate([head, dist[:, TILE:]], axis=1)
        skewed.append(pieces_of(head))
    lags = []
    for block in range(tiles):
        b = tiles - 1 - block
        span = (block + 1) * TILE
        lagged = add_dots(late, skewed[b])
        if block > 0:
            more = add_dots(early, skewed[b + 1])
            lagged = jnp.concatenate([lagged[:, :TILE], lagged[:, TILE:] + more], axis=1)
        lags.append(pltpu.roll(lagged, (1 + span - TILE) % span, 1, stride=1, stride_axis=0))
    full, pairs = packed_blocks(tiles)
    values = [lags[b][:, c * TILE : (c + 1) * TILE] for b, c in full]
    for one, two in pairs:
        values.append(jnp.where(lane < sub, lags[one][:, -TILE:], lags[two][:, -TILE:].T))
    for at, value in enumerate(values):
        side, slot = at // (len(values) // 2), at % (len(values) // 2)

        @pl.when(half == side)
        def _(value=value, slot=slot):
            keep_ref[slot * TILE : (slot + 1) * TILE, :] = value

        @pl.when(half != side)
        def _(value=value, slot=slot):
            send_ref[slot * TILE : (slot + 1) * TILE, :] = value


def quarter_kernel(chunk, keep_ref, got_ref, *outs):
    quad = device_places()[1]
    for mask in range(4):
        rows = pl.ds(pl.multiple_of((quad ^ mask) * chunk, 8), chunk)
        outs[mask][...] = keep_ref[rows, :] + got_ref[rows, :]


def split(x):
    high = x.astype(bf16)
    return high, (x - high.astype(f32)).astype(bf16)


def split_dot(a, b, contract=(((1,), (0,)), ((), ()))):
    a_high, a_low = split(a)
    b_high, b_low = split(b)
    rows = a.shape[0]
    stacked = jnp.concatenate([a_high, a_low], axis=0)
    first = lax.dot_general(stacked, b_high, contract, preferred_element_type=f32)
    second = lax.dot_general(a_high, b_low, contract, preferred_element_type=f32)
    return first[:rows] + (first[rows:] + second)


def inverse_factor(small):
    size = small.shape[0]
    sub = lax.broadcasted_iota(jnp.int32, (size, size), 0)
    lane = lax.broadcasted_iota(jnp.int32, (size, size), 1)
    eye = (sub == lane).astype(f32)
    work = jnp.concatenate([small, eye], axis=1)
    wide = work.shape
    below = lax.broadcasted_iota(jnp.int32, wide, 0)
    for first in range(0, size, PANEL):
        columns = [
            jnp.broadcast_to(work[:, first + a : first + a + 1], wide) for a in range(PANEL)
        ]
        for a in range(PANEL):
            k = first + a
            if k == size - 1:
                break
            scale = columns[a] / columns[a][k : k + 1, :]
            scale = jnp.where(below > k, scale, 0.0)
            for b in range(a + 1, PANEL):
                columns[b] = columns[b] - scale * columns[b][k : k + 1, :]
            work = work - scale * work[k : k + 1, :]
    pivots = jnp.sum(work[:, :size] * eye, axis=1, keepdims=True)
    begin = jnp.sum(small * eye, axis=1, keepdims=True)
    return work[:, size:] * lax.rsqrt(pivots), jnp.min(pivots / begin)


def finish_kernel(points, tiles, chunk, snaps, *refs):
    pieces, start_ref = refs[:8], refs[8]
    out_ref, packed_ref, high_ref, low_ref, wide_ref = refs[9:]
    half, quad, row_place, _ = device_places()
    for side in range(2):
        for mask in range(4):
            begin = pl.multiple_of((half ^ side) * (4 * chunk) + (quad ^ mask) * chunk, 8)
            packed_ref[pl.ds(begin, chunk), :] = pieces[side * 4 + mask][...]
    rows = snaps // 4
    sub = lax.broadcasted_iota(jnp.int32, (TILE, TILE), 0)
    lane = lax.broadcasted_iota(jnp.int32, (TILE, TILE), 1)
    full, pairs = packed_blocks(tiles)

    def factor(counts):
        return -1.0 / (counts.astype(f32) * (points * kernel_spread))

    def keep(value, block, c):
        high, low = split(value)
        high_ref[block * TILE : (block + 1) * TILE, c * TILE : (c + 1) * TILE] = high
        low_ref[block * TILE : (block + 1) * TILE, c * TILE : (c + 1) * TILE] = low

    for at, (block, c) in enumerate(full):
        columns = c * TILE + lane[:1, :]
        scale = factor(jnp.minimum(columns, LAGS - 1) + 1)
        value = jnp.exp(packed_ref[at * TILE : (at + 1) * TILE, :] * scale)
        keep(value, block, c)
        keep(value.T, c, block)
    for at, (one, two) in enumerate(pairs):
        shared = packed_ref[(len(full) + at) * TILE : (len(full) + at + 1) * TILE, :]
        swapped = shared.T
        for block, lagged in (
            (one, jnp.where(lane < sub, shared, swapped)),
            (two, jnp.where(lane > sub, shared, swapped)),
        ):
            counts = jnp.minimum(block * TILE + jnp.minimum(sub, lane), LAGS - 1) + 1
            lagged = jnp.where(lane == sub, 0.0, lagged)
            keep(jnp.exp(lagged * factor(counts)), block, block)
    ones = jnp.ones((16, snaps), bf16)
    degrees = jnp.dot(ones, high_ref[...], preferred_element_type=f32)
    degrees = degrees + jnp.dot(ones, low_ref[...], preferred_element_type=f32)
    inverse = 1.0 / degrees[0:1, :]
    scales = lax.sqrt(inverse)
    vecs = start_ref.shape[0]
    start = start_ref[...]

    def apply(x):
        x_high, x_low = split(x)
        stacked = jnp.concatenate([x_high, x_low], axis=0)
        first = jnp.dot(stacked, high_ref[...], preferred_element_type=f32)
        second = jnp.dot(x_high, low_ref[...], preferred_element_type=f32)
        return first[:vecs] + (first[vecs:] + second)

    across = (((1,), (1,)), ((), ()))

    def rounds(x, least, times):
        x = apply(x * scales)
        for _ in range(times - 1):
            x = apply(x * inverse)
        x = x * scales
        factor, ratio = inverse_factor(split_dot(x, x, across))
        return split_dot(factor, x), jnp.minimum(least, ratio)

    def loop(times):
        return lax.fori_loop(
            0,
            ITERS // times,
            lambda _, c: rounds(c[0], c[1], times),
            (start, f32(1.0)),
            unroll=times == 3,
        )

    basis, least = loop(3)
    wide_ref[...] = basis

    @pl.when(jnp.logical_not(least > 1e-4))
    def _():
        wide_ref[...] = loop(1)[0]

    basis = wide_ref[...]
    eye_sub = lax.broadcasted_iota(jnp.int32, (vecs, vecs), 0)
    eye_lane = lax.broadcasted_iota(jnp.int32, (vecs, vecs), 1)
    error = split_dot(basis, basis, across) - (eye_sub == eye_lane).astype(f32)
    weight = jnp.where(eye_sub > eye_lane, 1.0, jnp.where(eye_sub == eye_lane, 0.5, 0.0))
    wide_ref[...] = (basis - split_dot(error * weight, basis)) * math.sqrt(snaps)
    out_ref[...] = wide_ref[:, pl.ds(pl.multiple_of(row_place * rows, TILE), rows)]


def packed_body(points, snapshots, start_block):
    cols, feats = lax.axis_size("col"), lax.axis_size("feat")
    rows_total = lax.axis_size("row")
    members = rows_total * cols
    shard_rows, shard_points = snapshots.shape
    width = shard_points // members
    snaps = shard_rows * members
    tiles = snaps // TILE
    vecs = start_block.shape[1]
    steps = ring_steps(rows_total, cols)
    cuts = {}
    for group in ((1,), tuple(range(2, members)) + (0,)):
        chosen = [steps[step] for step in group]
        outs = pl.pallas_call(
            functools.partial(cut_kernel, chosen, rows_total, cols, width),
            out_shape=[pltpu.VMEM((shard_rows, width), bf16)] * len(group),
            in_specs=[any_spec()],
            out_specs=[vmem_spec()] * len(group),
            scratch_shapes=[pltpu.SemaphoreType.DMA((len(group),))],
            name="cut",
        )(snapshots)
        cuts.update(zip(group, outs))
    received = [cuts[0]]
    for step in range(1, members):
        shift, mask = steps[step]
        pairs = []
        for row in range(rows_total):
            for col in range(cols):
                there = (row + shift) % rows_total * cols + (col ^ mask)
                pairs.append((row * cols + col, there))
        received.append(lax.ppermute(cuts[step], ("row", "col"), pairs))
    turned = start_block.T
    starts = [turned] + [xor_permute(turned, "row", mask) for mask in range(1, 4)]

    full, shared = packed_blocks(tiles)
    total = (len(full) + len(shared)) * TILE
    side = total // 2
    chunk = side // 4
    keep, send, begin = pl.pallas_call(
        functools.partial(gram_kernel, steps, rows_total, cols, shard_rows),
        out_shape=[pltpu.VMEM((side, TILE), f32)] * 2 + [pltpu.VMEM((vecs, snaps), f32)],
        in_specs=[vmem_spec()] * (members + 4),
        out_specs=[vmem_spec()] * 3,
        scratch_shapes=[pltpu.VMEM((snaps, width), bf16)],
        name="gram",
    )(*[near(x) for x in received + starts])
    got = xor_permute(send, "feat", 1)
    quarters = pl.pallas_call(
        functools.partial(quarter_kernel, chunk),
        out_shape=[pltpu.VMEM((chunk, TILE), f32)] * 4,
        in_specs=[vmem_spec()] * 2,
        out_specs=[vmem_spec()] * 4,
        name="quarter",
    )(near(keep), near(got))
    mine = quarters[0]
    arrived = {mask: quad_permute(quarters[mask], mask) for mask in (3, 1, 2)}
    mine = (mine + arrived[1]) + (arrived[2] + arrived[3])
    others = {mask: xor_permute(mine, "row", mask) for mask in (1, 3, 2)}
    mine = (mine + others[1]) + (others[2] + others[3])
    pieces = [mine] + [quad_permute(mine, mask) for mask in range(1, 4)]
    pieces = pieces + [xor_permute(piece, "feat", 1) for piece in pieces]
    basis = pl.pallas_call(
        functools.partial(finish_kernel, float(points), tiles, chunk, snaps),
        out_shape=jax.ShapeDtypeStruct((vecs, snaps // rows_total), f32),
        in_specs=[vmem_spec()] * 9,
        out_specs=vmem_spec(),
        scratch_shapes=[
            pltpu.VMEM((total, TILE), f32),
            pltpu.VMEM((snaps, snaps), bf16),
            pltpu.VMEM((snaps, snaps), bf16),
            pltpu.VMEM((vecs, snaps), f32),
        ],
        name="finish",
    )(*[near(x) for x in pieces + [begin]])
    return basis.T


def solution(mesh):
    sizes = dict(mesh.shape)
    placed = (P(("row", "col"), "feat"), P("row", None))

    def run(snapshots, start_block):
        snaps, points = snapshots.shape
        members = sizes["row"] * sizes["col"]
        tiles = snaps // TILE
        packs = (
            sizes["row"] == 4
            and sizes["col"] == 2
            and sizes["feat"] == 4
            and snaps % (TILE * sizes["row"]) == 0
            and points % (TILE * members * sizes["feat"]) == 0
            and (tiles * tiles // 2) % 2 == 0
            and snaps <= 1024
        )
        body = packed_body if packs else spread_body
        mapped = jax.shard_map(
            functools.partial(body, points),
            mesh=mesh,
            in_specs=placed,
            out_specs=P("row", None),
            check_vma=False,
        )
        return mapped(snapshots, start_block)

    return run
```

```python
import functools
import math

import jax
import jax.numpy as jnp
from jax import lax
from jax.experimental import pallas as pl
from jax.experimental.pallas import tpu as pltpu
from jax.sharding import PartitionSpec as P

LAGS = 128
ITERS = 6
TILE = 128
PANEL = 16


kernel_spread = 0.25
highest = lax.Precision.HIGHEST
f32 = jnp.float32
bf16 = jnp.bfloat16


def broadcast(x, axis, root):
    mine = lax.axis_index(axis) == root
    return lax.psum(jnp.where(mine, x, jnp.zeros_like(x)), axis)


def shifted(x, axis, by):
    length = lax.axis_size(axis)
    pairs = [(i, i + by) for i in range(length) if 0 <= i + by < length]
    return lax.ppermute(x, axis, pairs)


def diagonal_window(extended, lag_count):
    running = None
    offset = 0
    partial_sum = extended
    levels = lag_count.bit_length()
    for level in range(levels):
        stride = 1 << level
        if lag_count & stride:
            running = partial_sum
            offset = offset + stride
        if level + 1 < levels:
            partial_sum = partial_sum[:-stride, :-stride] + partial_sum[stride:, stride:]
    return running


def orthonormal(product, gram_sum):
    factor = jnp.linalg.cholesky(gram_sum)
    return jax.scipy.linalg.solve_triangular(factor, product.T, lower=True).T


def square_norms(fields):
    widened = fields.astype(f32)
    return jnp.sum(widened * widened, axis=1)


def spread_body(points, snapshots, start_block):
    row_total = lax.axis_size("row")
    col_total = lax.axis_size("col")
    row_place = lax.axis_index("row")
    col_place = lax.axis_index("col")
    shard_rows = snapshots.shape[0]
    block_rows = shard_rows * col_total
    pairing = row_total // col_total
    block_cols = block_rows * pairing
    own_rows = lax.all_gather(snapshots, "col", axis=0, tiled=True)
    own_norms = square_norms(own_rows)
    members = []
    for member in range(pairing):
        members.append(broadcast(own_rows, "row", pairing * col_place + member))
    col_data = jnp.concatenate(members, axis=0)
    col_norms = square_norms(col_data)
    products = lax.dot_general(
        own_rows, col_data, (((1,), (1,)), ((), ())), preferred_element_type=f32
    )
    partial_dist = own_norms[:, None] + col_norms[None, :] - 2.0 * products
    distance = lax.psum(partial_dist, "feat")
    rim_width = LAGS - 1
    top_rim = shifted(distance[block_rows - rim_width :], "row", 1)
    upper = jnp.concatenate([top_rim, distance], axis=0)
    left_side = shifted(upper[:, block_cols - rim_width :], "col", 1)
    extended = jnp.concatenate([left_side, upper], axis=1)
    lagged = diagonal_window(extended, LAGS)
    row_ids = row_place * block_rows + lax.broadcasted_iota(jnp.int32, (block_rows, block_cols), 0)
    col_ids = col_place * block_cols + lax.broadcasted_iota(jnp.int32, (block_rows, block_cols), 1)
    counts = jnp.minimum(jnp.minimum(row_ids, col_ids), rim_width) + 1
    kernel = jnp.exp(-(lagged / (counts.astype(f32) * points)) / kernel_spread)
    row_degree = lax.psum(jnp.sum(kernel, axis=1), "col")
    every_degree = lax.all_gather(row_degree, "row", axis=0, tiled=True)
    col_degree = lax.dynamic_slice_in_dim(every_degree, col_place * block_cols, block_cols)
    markov = kernel * lax.rsqrt(row_degree)[:, None] * lax.rsqrt(col_degree)[None, :]
    basis = start_block
    for rounds in range(ITERS // 2):
        product = lax.dot_general(
            markov,
            basis,
            (((0,), (0,)), ((), ())),
            precision=highest,
            preferred_element_type=f32,
        )
        summed_cols = lax.psum(product, "row")
        row_product = jnp.dot(markov, summed_cols, precision=highest, preferred_element_type=f32)
        summed_rows = lax.psum(row_product, "col")
        local_gram = jnp.dot(
            summed_rows.T, summed_rows, precision=highest, preferred_element_type=f32
        )
        gram_rows = lax.psum(local_gram, "row")
        basis = orthonormal(summed_rows, gram_rows)
    return basis * math.sqrt(row_total * block_rows)


def any_spec():
    return pl.BlockSpec(memory_space=pl.ANY)


def vmem_spec():
    return pl.BlockSpec(memory_space=pltpu.VMEM)


def near(x):
    return pltpu.with_memory_space_constraint(x, pltpu.VMEM)


def xor_permute(x, axis, mask):
    return lax.ppermute(x, axis, [(i, i ^ mask) for i in range(lax.axis_size(axis))])


def quad_permute(x, mask):
    cols, feats = lax.axis_size("col"), lax.axis_size("feat")
    pairs = []
    for col in range(cols):
        for feat in range(feats):
            there = (col ^ (mask >> 1)) * feats + (feat ^ ((mask & 1) * (feats // 2)))
            pairs.append((col * feats + feat, there))
    return lax.ppermute(x, ("col", "feat"), pairs)


def packed_blocks(tiles):
    full = [(b, c) for b in range(tiles) for c in range(b)]
    return full, [(b, b + 1) for b in range(0, tiles, 2)]


def ring_steps(rows, cols):
    shifts = [rows // 2, 1, rows - 1]
    steps = [(a, (n + turn) % cols) for turn in range(cols) for n, a in enumerate(shifts)]
    return [(0, 0)] + steps + [(0, mask) for mask in range(1, cols)]


def device_places():
    row, col, feat = lax.axis_index("row"), lax.axis_index("col"), lax.axis_index("feat")
    return feat & 1, col * 2 + (feat >> 1), row, col


def cut_kernel(steps, rows_total, cols, width, x_ref, *refs):
    members = len(steps)
    outs, sems = refs[:members], refs[members]
    _, _, row, col = device_places()
    copies = []
    for step, (shift, mask) in enumerate(steps):
        there = lax.rem(row + shift, rows_total) * cols + (col ^ mask)
        begin = pl.multiple_of(there * width, TILE)
        copies.append(
            pltpu.make_async_copy(x_ref.at[:, pl.ds(begin, width)], outs[step], sems.at[step])
        )
    for copy in copies:
        copy.start()
    for copy in copies:
        copy.wait()


def pieces_of(whole):
    high = whole.astype(bf16)
    rest = whole - high.astype(f32)
    middle = rest.astype(bf16)
    return high, middle, (rest - middle.astype(f32)).astype(bf16)


def add_dots(weights, pieces):
    total = None
    for piece in pieces:
        term = jnp.dot(weights, piece, preferred_element_type=f32)
        total = term if total is None else total + term
    return total


def gram_kernel(steps, rows_total, cols, rows, *refs):
    members = len(steps)
    received, starts = refs[:members], refs[members : members + 2]
    keep_ref, send_ref, begin_ref, data_ref = refs[members + 2 :]
    half, _, row_place, col_place = device_places()
    for step, (shift, mask) in enumerate(steps):
        source = lax.rem(row_place + (rows_total - shift), rows_total) * cols + (col_place ^ mask)
        data_ref[pl.ds(pl.multiple_of(source * rows, rows), rows), :] = received[step][...]
    vecs = starts[0].shape[0]
    for mask in range(2):
        begin_ref[mask * vecs : (mask + 1) * vecs, :] = starts[mask][...]
    tiles = members * rows // TILE
    sub = lax.broadcasted_iota(jnp.int32, (TILE, TILE), 0)
    lane = lax.broadcasted_iota(jnp.int32, (TILE, TILE), 1)
    anti = sub + lane == TILE - 1
    flip = anti.astype(bf16)
    contract = (((1,), (1,)), ((), ()))
    strips, row_norms, col_norms = [], [], []
    for b in range(tiles):
        mirror = tiles - 1 - b
        block = data_ref[mirror * TILE : (mirror + 1) * TILE, :]
        turned = jnp.dot(flip, block, preferred_element_type=f32).astype(bf16)
        prods = lax.dot_general(
            turned, data_ref[: (mirror + 1) * TILE, :], contract, preferred_element_type=f32
        )
        strips.append(prods)
        own = jnp.where(anti, prods[:, mirror * TILE :], 0.0)
        row_norms.append(jnp.sum(own, axis=1, keepdims=True))
        col_norms.append(jnp.sum(own, axis=0, keepdims=True))
    norms = jnp.concatenate(col_norms[::-1], axis=1)
    late = (sub + lane >= TILE - 1).astype(bf16)
    early = (sub + lane < TILE - 1).astype(bf16)
    skewed = []
    for b in range(tiles):
        span = (tiles - b) * TILE
        dist = row_norms[b] + norms[:, :span] - 2.0 * strips[b]
        dist = pltpu.roll(dist, 0, 1, stride=1, stride_axis=0)
        head = jnp.where(lane >= sub, dist[:, :TILE], 0.0)
        if span > TILE:
            head = jnp.concatenate([head, dist[:, TILE:]], axis=1)
        skewed.append(pieces_of(head))
    lags = []
    for block in range(tiles):
        b = tiles - 1 - block
        span = (block + 1) * TILE
        lagged = add_dots(late, skewed[b])
        if block > 0:
            more = add_dots(early, skewed[b + 1])
            lagged = jnp.concatenate([lagged[:, :TILE], lagged[:, TILE:] + more], axis=1)
        lags.append(pltpu.roll(lagged, (1 + span - TILE) % span, 1, stride=1, stride_axis=0))
    full, pairs = packed_blocks(tiles)
    values = [lags[b][:, c * TILE : (c + 1) * TILE] for b, c in full]
    for one, two in pairs:
        values.append(jnp.where(lane < sub, lags[one][:, -TILE:], lags[two][:, -TILE:].T))
    for at, value in enumerate(values):
        side, slot = at // (len(values) // 2), at % (len(values) // 2)

        @pl.when(half == side)
        def _(value=value, slot=slot):
            keep_ref[slot * TILE : (slot + 1) * TILE, :] = value

        @pl.when(half != side)
        def _(value=value, slot=slot):
            send_ref[slot * TILE : (slot + 1) * TILE, :] = value


def quarter_kernel(chunk, keep_ref, got_ref, *outs):
    quad = device_places()[1]
    for mask in range(4):
        rows = pl.ds(pl.multiple_of((quad ^ mask) * chunk, 8), chunk)
        outs[mask][...] = keep_ref[rows, :] + got_ref[rows, :]


def sum_kernel(*refs):
    one, two, three, four, begin_ref, out_ref, pass_ref = refs
    out_ref[...] = (one[...] + two[...]) + (three[...] + four[...])
    pass_ref[...] = begin_ref[...]


def split(x):
    high = x.astype(bf16)
    return high, (x - high.astype(f32)).astype(bf16)


def split_dot(a, b, contract=(((1,), (0,)), ((), ()))):
    a_high, a_low = split(a)
    b_high, b_low = split(b)
    rows = a.shape[0]
    stacked = jnp.concatenate([a_high, a_low], axis=0)
    first = lax.dot_general(stacked, b_high, contract, preferred_element_type=f32)
    second = lax.dot_general(a_high, b_low, contract, preferred_element_type=f32)
    return first[:rows] + (first[rows:] + second)


def inverse_factor(small):
    size = small.shape[0]
    sub = lax.broadcasted_iota(jnp.int32, (size, size), 0)
    lane = lax.broadcasted_iota(jnp.int32, (size, size), 1)
    eye = (sub == lane).astype(f32)
    work = jnp.concatenate([small, eye], axis=1)
    wide = work.shape
    below = lax.broadcasted_iota(jnp.int32, wide, 0)
    for first in range(0, size, PANEL):
        columns = [
            jnp.broadcast_to(work[:, first + a : first + a + 1], wide) for a in range(PANEL)
        ]
        for a in range(PANEL):
            k = first + a
            if k == size - 1:
                break
            scale = columns[a] / columns[a][k : k + 1, :]
            scale = jnp.where(below > k, scale, 0.0)
            for b in range(a + 1, PANEL):
                columns[b] = columns[b] - scale * columns[b][k : k + 1, :]
            work = work - scale * work[k : k + 1, :]
    pivots = jnp.sum(work[:, :size] * eye, axis=1, keepdims=True)
    begin = jnp.sum(small * eye, axis=1, keepdims=True)
    return work[:, size:] * lax.rsqrt(pivots), jnp.min(pivots / begin)


def finish_kernel(points, tiles, chunk, snaps, *refs):
    pieces, begins = refs[:8], refs[8:10]
    out_ref, packed_ref, high_ref, low_ref, wide_ref = refs[10:]
    half, quad, row_place, _ = device_places()
    for side in range(2):
        for mask in range(4):
            begin = pl.multiple_of((half ^ side) * (4 * chunk) + (quad ^ mask) * chunk, 8)
            packed_ref[pl.ds(begin, chunk), :] = pieces[side * 4 + mask][...]
    rows = snaps // 4
    sub = lax.broadcasted_iota(jnp.int32, (TILE, TILE), 0)
    lane = lax.broadcasted_iota(jnp.int32, (TILE, TILE), 1)
    full, pairs = packed_blocks(tiles)

    def factor(counts):
        return -1.0 / (counts.astype(f32) * (points * kernel_spread))

    def keep(value, block, c):
        high, low = split(value)
        high_ref[block * TILE : (block + 1) * TILE, c * TILE : (c + 1) * TILE] = high
        low_ref[block * TILE : (block + 1) * TILE, c * TILE : (c + 1) * TILE] = low

    for at, (block, c) in enumerate(full):
        columns = c * TILE + lane[:1, :]
        scale = factor(jnp.minimum(columns, LAGS - 1) + 1)
        value = jnp.exp(packed_ref[at * TILE : (at + 1) * TILE, :] * scale)
        keep(value, block, c)
        keep(value.T, c, block)
    for at, (one, two) in enumerate(pairs):
        shared = packed_ref[(len(full) + at) * TILE : (len(full) + at + 1) * TILE, :]
        swapped = shared.T
        for block, lagged in (
            (one, jnp.where(lane < sub, shared, swapped)),
            (two, jnp.where(lane > sub, shared, swapped)),
        ):
            counts = jnp.minimum(block * TILE + jnp.minimum(sub, lane), LAGS - 1) + 1
            lagged = jnp.where(lane == sub, 0.0, lagged)
            keep(jnp.exp(lagged * factor(counts)), block, block)
    ones = jnp.ones((16, snaps), bf16)
    degrees = jnp.dot(ones, high_ref[...], preferred_element_type=f32)
    degrees = degrees + jnp.dot(ones, low_ref[...], preferred_element_type=f32)
    inverse = 1.0 / degrees[0:1, :]
    scales = lax.sqrt(inverse)
    vecs = begins[0].shape[0] // 2
    for mask in range(4):
        begin = pl.multiple_of((row_place ^ mask) * rows, TILE)
        half_rows = slice(mask % 2 * vecs, (mask % 2 + 1) * vecs)
        wide_ref[:, pl.ds(begin, rows)] = begins[mask // 2][half_rows, :]
    start = wide_ref[...]

    def apply(x):
        x_high, x_low = split(x)
        stacked = jnp.concatenate([x_high, x_low], axis=0)
        first = jnp.dot(stacked, high_ref[...], preferred_element_type=f32)
        second = jnp.dot(x_high, low_ref[...], preferred_element_type=f32)
        return first[:vecs] + (first[vecs:] + second)

    across = (((1,), (1,)), ((), ()))

    def rounds(x, least, times):
        x = apply(x * scales)
        for _ in range(times - 1):
            x = apply(x * inverse)
        x = x * scales
        factor, ratio = inverse_factor(split_dot(x, x, across))
        return split_dot(factor, x), jnp.minimum(least, ratio)

    def loop(times):
        return lax.fori_loop(
            0,
            ITERS // times,
            lambda _, c: rounds(c[0], c[1], times),
            (start, f32(1.0)),
            unroll=times == 3,
        )

    basis, least = loop(3)
    wide_ref[...] = basis

    @pl.when(jnp.logical_not(least > 1e-4))
    def _():
        wide_ref[...] = loop(1)[0]

    basis = wide_ref[...]
    eye_sub = lax.broadcasted_iota(jnp.int32, (vecs, vecs), 0)
    eye_lane = lax.broadcasted_iota(jnp.int32, (vecs, vecs), 1)
    error = split_dot(basis, basis, across) - (eye_sub == eye_lane).astype(f32)
    weight = jnp.where(eye_sub > eye_lane, 1.0, jnp.where(eye_sub == eye_lane, 0.5, 0.0))
    wide_ref[...] = (basis - split_dot(error * weight, basis)) * math.sqrt(snaps)
    out_ref[...] = wide_ref[:, pl.ds(pl.multiple_of(row_place * rows, TILE), rows)]


def packed_body(points, snapshots, start_block):
    cols, feats = lax.axis_size("col"), lax.axis_size("feat")
    rows_total = lax.axis_size("row")
    members = rows_total * cols
    shard_rows, shard_points = snapshots.shape
    width = shard_points // members
    snaps = shard_rows * members
    tiles = snaps // TILE
    vecs = start_block.shape[1]
    steps = ring_steps(rows_total, cols)
    cuts = {}
    for group in ((1,), tuple(range(2, members)) + (0,)):
        chosen = [steps[step] for step in group]
        outs = pl.pallas_call(
            functools.partial(cut_kernel, chosen, rows_total, cols, width),
            out_shape=[pltpu.VMEM((shard_rows, width), bf16)] * len(group),
            in_specs=[any_spec()],
            out_specs=[vmem_spec()] * len(group),
            scratch_shapes=[pltpu.SemaphoreType.DMA((len(group),))],
            name="cut",
        )(snapshots)
        cuts.update(zip(group, outs))
    received = [cuts[0]]
    for step in range(1, members):
        shift, mask = steps[step]
        pairs = []
        for row in range(rows_total):
            for col in range(cols):
                there = (row + shift) % rows_total * cols + (col ^ mask)
                pairs.append((row * cols + col, there))
        received.append(lax.ppermute(cuts[step], ("row", "col"), pairs))
    turned = start_block.T
    starts = [turned, xor_permute(turned, "row", 1)]

    full, shared = packed_blocks(tiles)
    total = (len(full) + len(shared)) * TILE
    side = total // 2
    chunk = side // 4
    keep, send, begin = pl.pallas_call(
        functools.partial(gram_kernel, steps, rows_total, cols, shard_rows),
        out_shape=[pltpu.VMEM((side, TILE), f32)] * 2 + [pltpu.VMEM((2 * vecs, snaps // rows_total), f32)],
        in_specs=[vmem_spec()] * (members + 2),
        out_specs=[vmem_spec()] * 3,
        scratch_shapes=[pltpu.VMEM((snaps, width), bf16)],
        name="gram",
    )(*[near(x) for x in received + starts])
    got = xor_permute(send, "feat", 1)
    begins = [begin, xor_permute(begin, "row", 2)]
    quarters = pl.pallas_call(
        functools.partial(quarter_kernel, chunk),
        out_shape=[pltpu.VMEM((chunk, TILE), f32)] * 4,
        in_specs=[vmem_spec()] * 2,
        out_specs=[vmem_spec()] * 4,
        name="quarter",
    )(near(keep), near(got))
    mine = quarters[0]
    arrived = {mask: quad_permute(quarters[mask], mask) for mask in (3, 1, 2)}
    mine, begins[1] = pl.pallas_call(
        sum_kernel,
        out_shape=[pltpu.VMEM((chunk, TILE), f32), pltpu.VMEM(begin.shape, f32)],
        in_specs=[vmem_spec()] * 5,
        out_specs=[vmem_spec()] * 2,
        name="sum",
    )(*[near(x) for x in (mine, arrived[3], arrived[1], arrived[2], begins[1])])
    others = {mask: xor_permute(mine, "row", mask) for mask in (1, 3, 2)}
    mine = (mine + others[1]) + (others[3] + others[2])
    pieces = [mine] + [quad_permute(mine, mask) for mask in range(1, 4)]
    pieces = pieces + [xor_permute(piece, "feat", 1) for piece in pieces]
    basis = pl.pallas_call(
        functools.partial(finish_kernel, float(points), tiles, chunk, snaps),
        out_shape=jax.ShapeDtypeStruct((vecs, snaps // rows_total), f32),
        in_specs=[vmem_spec()] * 10,
        out_specs=vmem_spec(),
        scratch_shapes=[
            pltpu.VMEM((total, TILE), f32),
            pltpu.VMEM((snaps, snaps), bf16),
            pltpu.VMEM((snaps, snaps), bf16),
            pltpu.VMEM((vecs, snaps), f32),
        ],
        name="finish",
    )(*[near(x) for x in pieces + begins])
    return basis.T


def solution(mesh):
    sizes = dict(mesh.shape)
    placed = (P(("row", "col"), "feat"), P("row", None))

    def run(snapshots, start_block):
        snaps, points = snapshots.shape
        members = sizes["row"] * sizes["col"]
        tiles = snaps // TILE
        packs = (
            sizes["row"] == 4
            and sizes["col"] == 2
            and sizes["feat"] == 4
            and snaps % (TILE * sizes["row"]) == 0
            and points % (TILE * members * sizes["feat"]) == 0
            and (tiles * tiles // 2) % 2 == 0
            and snaps <= 1024
        )
        body = packed_body if packs else spread_body
        mapped = jax.shard_map(
            functools.partial(body, points),
            mesh=mesh,
            in_specs=placed,
            out_specs=P("row", None),
            check_vma=False,
        )
        return mapped(snapshots, start_block)

    return run
```

```python
import functools
import math

import jax
import jax.numpy as jnp
from jax import lax
from jax.experimental import pallas as pl
from jax.experimental.pallas import tpu as pltpu
from jax.sharding import PartitionSpec as P


LAGS = 128
ITERS = 6
TILE = 128
PANEL = 16


kernel_spread = 0.25
highest = lax.Precision.HIGHEST
f32 = jnp.float32
bf16 = jnp.bfloat16


def broadcast(x, axis, root):
    mine = lax.axis_index(axis) == root
    return lax.psum(jnp.where(mine, x, jnp.zeros_like(x)), axis)


def shifted(x, axis, by):
    length = lax.axis_size(axis)
    pairs = [(i, i + by) for i in range(length) if 0 <= i + by < length]
    return lax.ppermute(x, axis, pairs)


def diagonal_window(extended, lag_count):
    running = None
    partial_sum = extended
    levels = lag_count.bit_length()
    for level in range(levels):
        stride = 1 << level
        if lag_count & stride:
            running = partial_sum
        if level + 1 < levels:
            partial_sum = partial_sum[:-stride, :-stride] + partial_sum[stride:, stride:]
    return running


def orthonormal(product, gram_sum):
    factor = jnp.linalg.cholesky(gram_sum)
    return jax.scipy.linalg.solve_triangular(factor, product.T, lower=True).T


def square_norms(fields):
    widened = fields.astype(f32)
    return jnp.sum(widened * widened, axis=1)


def spread_body(points, snapshots, start_block):
    row_total = lax.axis_size("row")
    col_total = lax.axis_size("col")
    row_place = lax.axis_index("row")
    col_place = lax.axis_index("col")
    shard_rows = snapshots.shape[0]
    block_rows = shard_rows * col_total
    pairing = row_total // col_total
    block_cols = block_rows * pairing
    own_rows = lax.all_gather(snapshots, "col", axis=0, tiled=True)
    own_norms = square_norms(own_rows)
    members = []
    for member in range(pairing):
        members.append(broadcast(own_rows, "row", pairing * col_place + member))
    col_data = jnp.concatenate(members, axis=0)
    col_norms = square_norms(col_data)
    products = lax.dot_general(
        own_rows, col_data, (((1,), (1,)), ((), ())), preferred_element_type=f32
    )
    partial_dist = own_norms[:, None] + col_norms[None, :] - 2.0 * products
    distance = lax.psum(partial_dist, "feat")
    rim_width = LAGS - 1
    top_rim = shifted(distance[block_rows - rim_width :], "row", 1)
    upper = jnp.concatenate([top_rim, distance], axis=0)
    left_side = shifted(upper[:, block_cols - rim_width :], "col", 1)
    extended = jnp.concatenate([left_side, upper], axis=1)
    lagged = diagonal_window(extended, LAGS)
    row_ids = row_place * block_rows + lax.broadcasted_iota(jnp.int32, (block_rows, block_cols), 0)
    col_ids = col_place * block_cols + lax.broadcasted_iota(jnp.int32, (block_rows, block_cols), 1)
    counts = jnp.minimum(jnp.minimum(row_ids, col_ids), rim_width) + 1
    kernel = jnp.exp(-(lagged / (counts.astype(f32) * points)) / kernel_spread)
    row_degree = lax.psum(jnp.sum(kernel, axis=1), "col")
    every_degree = lax.all_gather(row_degree, "row", axis=0, tiled=True)
    col_degree = lax.dynamic_slice_in_dim(every_degree, col_place * block_cols, block_cols)
    markov = kernel * lax.rsqrt(row_degree)[:, None] * lax.rsqrt(col_degree)[None, :]
    basis = start_block
    for _ in range(ITERS // 2):
        product = lax.dot_general(
            markov,
            basis,
            (((0,), (0,)), ((), ())),
            precision=highest,
            preferred_element_type=f32,
        )
        summed_cols = lax.psum(product, "row")
        row_product = jnp.dot(markov, summed_cols, precision=highest, preferred_element_type=f32)
        summed_rows = lax.psum(row_product, "col")
        local_gram = jnp.dot(
            summed_rows.T, summed_rows, precision=highest, preferred_element_type=f32
        )
        gram_rows = lax.psum(local_gram, "row")
        basis = orthonormal(summed_rows, gram_rows)
    return basis * math.sqrt(row_total * block_rows)


def any_spec():
    return pl.BlockSpec(memory_space=pl.ANY)


def vmem_spec():
    return pl.BlockSpec(memory_space=pltpu.VMEM)


def near(x):
    return pltpu.with_memory_space_constraint(x, pltpu.VMEM)


def xor_permute(x, axis, mask):
    return lax.ppermute(x, axis, [(i, i ^ mask) for i in range(lax.axis_size(axis))])


def quad_permute(x, mask):
    cols, feats = lax.axis_size("col"), lax.axis_size("feat")
    pairs = []
    for col in range(cols):
        for feat in range(feats):
            there = (col ^ (mask >> 1)) * feats + (feat ^ ((mask & 1) * (feats // 2)))
            pairs.append((col * feats + feat, there))
    return lax.ppermute(x, ("col", "feat"), pairs)


def packed_blocks(tiles):
    full = [(b, c) for b in range(tiles) for c in range(b)]
    return full, [(b, b + 1) for b in range(0, tiles, 2)]


def ring_steps(rows, cols):
    shifts = [rows // 2, 1, rows - 1]
    steps = [(a, (n + turn) % cols) for turn in range(cols) for n, a in enumerate(shifts)]
    return [(0, 0)] + steps + [(0, mask) for mask in range(1, cols)]


def device_places():
    row, col, feat = lax.axis_index("row"), lax.axis_index("col"), lax.axis_index("feat")
    return feat & 1, col * 2 + (feat >> 1), row, col


def cut_kernel(steps, rows_total, cols, width, x_ref, *refs):
    members = len(steps)
    outs, sems = refs[:members], refs[members]
    parts = sems.shape[0] // members
    rows_each = x_ref.shape[0] // parts
    _, _, row, col = device_places()
    copies = []
    for step, (shift, mask) in enumerate(steps):
        there = lax.rem(row + shift, rows_total) * cols + (col ^ mask)
        begin = pl.multiple_of(there * width, TILE)
        for part in range(parts):
            rows = slice(part * rows_each, (part + 1) * rows_each)
            copies.append(
                pltpu.make_async_copy(
                    x_ref.at[rows, pl.ds(begin, width)],
                    outs[step].at[rows, :],
                    sems.at[step * parts + part],
                )
            )
    for copy in copies:
        copy.start()
    for copy in copies:
        copy.wait()


def pieces_of(whole):
    high = whole.astype(bf16)
    rest = whole - high.astype(f32)
    middle = rest.astype(bf16)
    return high, middle, (rest - middle.astype(f32)).astype(bf16)


def add_dots(weights, pieces):
    total = None
    for piece in pieces:
        term = jnp.dot(weights, piece, preferred_element_type=f32)
        total = term if total is None else total + term
    return total


def gram_kernel(steps, rows_total, cols, rows, *refs):
    members = len(steps)
    received, starts = refs[:members], refs[members : members + 2]
    keep_ref, send_ref, begin_ref, data_ref = refs[members + 2 :]
    half, _, row_place, col_place = device_places()
    for step, (shift, mask) in enumerate(steps):
        source = lax.rem(row_place + (rows_total - shift), rows_total) * cols + (col_place ^ mask)
        data_ref[pl.ds(pl.multiple_of(source * rows, rows), rows), :] = received[step][...]
    vecs = starts[0].shape[0]
    for mask in range(2):
        begin_ref[mask * vecs : (mask + 1) * vecs, :] = starts[mask][...]
    tiles = members * rows // TILE
    sub = lax.broadcasted_iota(jnp.int32, (TILE, TILE), 0)
    lane = lax.broadcasted_iota(jnp.int32, (TILE, TILE), 1)
    anti = sub + lane == TILE - 1
    flip = anti.astype(bf16)
    contract = (((1,), (1,)), ((), ()))
    strips, row_norms, col_norms = [], [], []
    for b in range(tiles):
        mirror = tiles - 1 - b
        block = data_ref[mirror * TILE : (mirror + 1) * TILE, :]
        turned = jnp.dot(flip, block, preferred_element_type=f32).astype(bf16)
        prods = lax.dot_general(
            turned, data_ref[: (mirror + 1) * TILE, :], contract, preferred_element_type=f32
        )
        strips.append(prods)
        own = jnp.where(anti, prods[:, mirror * TILE :], 0.0)
        row_norms.append(jnp.sum(own, axis=1, keepdims=True))
        col_norms.append(jnp.sum(own, axis=0, keepdims=True))
    norms = jnp.concatenate(col_norms[::-1], axis=1)
    late = (sub + lane >= TILE - 1).astype(bf16)
    early = (sub + lane < TILE - 1).astype(bf16)
    skewed = []
    for b in range(tiles):
        span = (tiles - b) * TILE
        dist = row_norms[b] + norms[:, :span] - 2.0 * strips[b]
        dist = pltpu.roll(dist, 0, 1, stride=1, stride_axis=0)
        head = jnp.where(lane >= sub, dist[:, :TILE], 0.0)
        if span > TILE:
            head = jnp.concatenate([head, dist[:, TILE:]], axis=1)
        skewed.append(pieces_of(head))
    lags = []
    for block in range(tiles):
        b = tiles - 1 - block
        span = (block + 1) * TILE
        lagged = add_dots(late, skewed[b])
        if block > 0:
            more = add_dots(early, skewed[b + 1])
            lagged = jnp.concatenate([lagged[:, :TILE], lagged[:, TILE:] + more], axis=1)
        lags.append(pltpu.roll(lagged, (1 + span - TILE) % span, 1, stride=1, stride_axis=0))
    full, pairs = packed_blocks(tiles)
    values = [lags[b][:, c * TILE : (c + 1) * TILE] for b, c in full]
    for one, two in pairs:
        values.append(jnp.where(lane < sub, lags[one][:, -TILE:], lags[two][:, -TILE:].T))
    count = len(values) // 2
    for slot in range(count):
        rows = slice(slot * TILE, (slot + 1) * TILE)
        keep_ref[rows, :] = jnp.where(half == 0, values[slot], values[count + slot])
        send_ref[rows, :] = jnp.where(half == 0, values[count + slot], values[slot])


def quarter_kernel(chunk, keep_ref, got_ref, *outs):
    quad = device_places()[1]
    for mask in range(4):
        rows = pl.ds(pl.multiple_of((quad ^ mask) * chunk, 8), chunk)
        outs[mask][...] = keep_ref[rows, :] + got_ref[rows, :]


def split(x):
    high = x.astype(bf16)
    return high, (x - high.astype(f32)).astype(bf16)


def split_dot(a, b, contract=(((1,), (0,)), ((), ()))):
    a_high, a_low = split(a)
    b_high, b_low = split(b)
    rows = a.shape[0]
    stacked = jnp.concatenate([a_high, a_low], axis=0)
    first = lax.dot_general(stacked, b_high, contract, preferred_element_type=f32)
    second = lax.dot_general(a_high, b_low, contract, preferred_element_type=f32)
    return first[:rows] + (first[rows:] + second)


def inverse_factor(small):
    size = small.shape[0]
    sub = lax.broadcasted_iota(jnp.int32, (size, size), 0)
    lane = lax.broadcasted_iota(jnp.int32, (size, size), 1)
    eye = (sub == lane).astype(f32)
    rest = jnp.concatenate([small, eye], axis=1)
    done = []
    for first in range(0, size, PANEL):
        wide = rest.shape
        below = lax.broadcasted_iota(jnp.int32, wide, 0)
        columns = [
            jnp.broadcast_to(rest[:, first + a : first + a + 1], wide) for a in range(PANEL)
        ]
        for a in range(min(PANEL, size - 1 - first)):
            scale = columns[a] * (1.0 / columns[a][a : a + 1, :])
            scale = jnp.where(below > a, scale, 0.0)
            for b in range(a + 1, PANEL):
                columns[b] = columns[b] - scale * columns[b][a : a + 1, :]
            rest = rest - scale * rest[a : a + 1, :]
        done.append(rest[:PANEL, :])
        rest = rest[PANEL:, :]
    work = jnp.concatenate(done, axis=0)
    pivots = jnp.sum(work[:, :size] * eye, axis=1, keepdims=True)
    begin = jnp.sum(small * eye, axis=1, keepdims=True)
    return work[:, size:] * lax.rsqrt(pivots), jnp.min(pivots / begin)


def finish_kernel(points, tiles, chunk, snaps, *refs):
    pieces, begins = refs[:8], refs[8:10]
    out_ref, packed_ref, high_ref, low_ref, wide_ref = refs[10:]
    half, quad, row_place, _ = device_places()
    for side in range(2):
        for mask in range(4):
            begin = pl.multiple_of((half ^ side) * (4 * chunk) + (quad ^ mask) * chunk, 8)
            packed_ref[pl.ds(begin, chunk), :] = pieces[side * 4 + mask][...]
    rows = snaps // 4
    sub = lax.broadcasted_iota(jnp.int32, (TILE, TILE), 0)
    lane = lax.broadcasted_iota(jnp.int32, (TILE, TILE), 1)
    full, pairs = packed_blocks(tiles)

    def factor(counts):
        return -1.0 / (counts.astype(f32) * (points * kernel_spread))

    def keep(value, block, c):
        high, low = split(value)
        high_ref[block * TILE : (block + 1) * TILE, c * TILE : (c + 1) * TILE] = high
        low_ref[block * TILE : (block + 1) * TILE, c * TILE : (c + 1) * TILE] = low

    for at, (block, c) in enumerate(full):
        columns = c * TILE + lane[:1, :]
        scale = factor(jnp.minimum(columns, LAGS - 1) + 1)
        value = jnp.exp(packed_ref[at * TILE : (at + 1) * TILE, :] * scale)
        keep(value, block, c)
        keep(value.T, c, block)
    for at, (one, two) in enumerate(pairs):
        shared = packed_ref[(len(full) + at) * TILE : (len(full) + at + 1) * TILE, :]
        swapped = shared.T
        for block, lagged in (
            (one, jnp.where(lane < sub, shared, swapped)),
            (two, jnp.where(lane > sub, shared, swapped)),
        ):
            counts = jnp.minimum(block * TILE + jnp.minimum(sub, lane), LAGS - 1) + 1
            lagged = jnp.where(lane == sub, 0.0, lagged)
            keep(jnp.exp(lagged * factor(counts)), block, block)
    ones = jnp.ones((16, snaps), bf16)
    degrees = jnp.dot(ones, high_ref[...], preferred_element_type=f32)
    degrees = degrees + jnp.dot(ones, low_ref[...], preferred_element_type=f32)
    inverse = 1.0 / degrees[0:1, :]
    scales = lax.sqrt(inverse)
    vecs = begins[0].shape[0] // 2
    for mask in range(4):
        begin = pl.multiple_of((row_place ^ mask) * rows, TILE)
        half_rows = slice(mask % 2 * vecs, (mask % 2 + 1) * vecs)
        wide_ref[:, pl.ds(begin, rows)] = begins[mask // 2][half_rows, :]
    start = wide_ref[...]

    def apply(x):
        x_high, x_low = split(x)
        stacked = jnp.concatenate([x_high, x_low], axis=0)
        first = jnp.dot(stacked, high_ref[...], preferred_element_type=f32)
        second = jnp.dot(x_high, low_ref[...], preferred_element_type=f32)
        return first[:vecs] + (first[vecs:] + second)

    across = (((1,), (1,)), ((), ()))

    def rounds(x, least, times):
        x = apply(x * scales)
        for _ in range(times - 1):
            x = apply(x * inverse)
        x = x * scales
        factor, ratio = inverse_factor(split_dot(x, x, across))
        return split_dot(factor, x), jnp.minimum(least, ratio)

    def loop(times):
        return lax.fori_loop(
            0,
            ITERS // times,
            lambda _, c: rounds(c[0], c[1], times),
            (start, f32(1.0)),
            unroll=times == 3,
        )

    basis, least = loop(3)
    wide_ref[...] = basis

    @pl.when(jnp.logical_not(least > 1e-4))
    def _():
        wide_ref[...] = loop(1)[0]

    basis = wide_ref[...]
    eye_sub = lax.broadcasted_iota(jnp.int32, (vecs, vecs), 0)
    eye_lane = lax.broadcasted_iota(jnp.int32, (vecs, vecs), 1)
    error = split_dot(basis, basis, across) - (eye_sub == eye_lane).astype(f32)
    weight = jnp.where(eye_sub > eye_lane, 1.0, jnp.where(eye_sub == eye_lane, 0.5, 0.0))
    wide_ref[...] = (basis - split_dot(error * weight, basis)) * math.sqrt(snaps)
    out_ref[...] = wide_ref[:, pl.ds(pl.multiple_of(row_place * rows, TILE), rows)]


def packed_body(points, snapshots, start_block):
    return packed_plan(points, snapshots, start_block)


def packed_plan(points, snapshots, start_block):
    cols = lax.axis_size("col")
    rows_total = lax.axis_size("row")
    members = rows_total * cols
    shard_rows, shard_points = snapshots.shape
    width = shard_points // members
    snaps = shard_rows * members
    tiles = snaps // TILE
    vecs = start_block.shape[1]
    steps = ring_steps(rows_total, cols)
    cuts = {}
    for group in ((1,), tuple(range(2, members)) + (0,)):
        chosen = [steps[step] for step in group]
        outs = pl.pallas_call(
            functools.partial(cut_kernel, chosen, rows_total, cols, width),
            out_shape=[pltpu.VMEM((shard_rows, width), bf16)] * len(group),
            in_specs=[any_spec()],
            out_specs=[vmem_spec()] * len(group),
            scratch_shapes=[pltpu.SemaphoreType.DMA((len(group) * (4 if len(group) == 1 else 1),))],
            name="cut",
        )(snapshots)
        cuts.update(zip(group, outs))
    received = [cuts[0]]
    for step in range(1, members):
        shift, mask = steps[step]
        pairs = []
        for row in range(rows_total):
            for col in range(cols):
                there = (row + shift) % rows_total * cols + (col ^ mask)
                pairs.append((row * cols + col, there))
        received.append(lax.ppermute(cuts[step], ("row", "col"), pairs))
    turned = start_block.T
    starts = [turned, xor_permute(turned, "row", 1)]

    full, shared = packed_blocks(tiles)
    total = (len(full) + len(shared)) * TILE
    side = total // 2
    chunk = side // 4
    keep, send, begin = pl.pallas_call(
        functools.partial(gram_kernel, steps, rows_total, cols, shard_rows),
        out_shape=[pltpu.VMEM((side, TILE), f32)] * 2 + [pltpu.VMEM((2 * vecs, snaps // rows_total), f32)],
        in_specs=[vmem_spec()] * (members + 2),
        out_specs=[vmem_spec()] * 3,
        scratch_shapes=[pltpu.VMEM((snaps, width), bf16)],
        name="gram",
    )(*[near(x) for x in received + starts])
    got = xor_permute(send, "feat", 1)
    begins = [begin, xor_permute(begin, "row", 2)]
    quarters = pl.pallas_call(
        functools.partial(quarter_kernel, chunk),
        out_shape=[pltpu.VMEM((chunk, TILE), f32)] * 4,
        in_specs=[vmem_spec()] * 2,
        out_specs=[vmem_spec()] * 4,
        name="quarter",
    )(near(keep), near(got))
    mine = quarters[0]
    arrived = {}
    for mask in (3, 1, 2):
        arrived[mask] = quad_permute(quarters[mask], mask)
    mine = (mine + arrived[3]) + (arrived[1] + arrived[2])
    others = {mask: xor_permute(mine, "row", mask) for mask in (1, 3, 2)}
    mine = (mine + others[1]) + (others[3] + others[2])
    pieces = [mine] + [quad_permute(mine, mask) for mask in range(1, 4)]
    pieces = pieces + [xor_permute(piece, "feat", 1) for piece in pieces]
    basis = pl.pallas_call(
        functools.partial(finish_kernel, float(points), tiles, chunk, snaps),
        out_shape=jax.ShapeDtypeStruct((vecs, snaps // rows_total), f32),
        in_specs=[vmem_spec()] * 10,
        out_specs=vmem_spec(),
        scratch_shapes=[
            pltpu.VMEM((total, TILE), f32),
            pltpu.VMEM((snaps, snaps), bf16),
            pltpu.VMEM((snaps, snaps), bf16),
            pltpu.VMEM((vecs, snaps), f32),
        ],
        name="finish",
    )(*[near(x) for x in pieces + begins])
    return basis.T


def solution(mesh):
    sizes = dict(mesh.shape)
    placed = (P(("row", "col"), "feat"), P("row", None))

    def run(snapshots, start_block):
        snaps, points = snapshots.shape
        members = sizes["row"] * sizes["col"]
        tiles = snaps // TILE
        packs = (
            sizes["row"] == 4
            and sizes["col"] == 2
            and sizes["feat"] == 4
            and snaps % (TILE * sizes["row"]) == 0
            and points % (TILE * members * sizes["feat"]) == 0
            and (tiles * tiles // 2) % 2 == 0
            and snaps <= 1024
        )
        body = packed_body if packs else spread_body
        mapped = jax.shard_map(
            functools.partial(body, points),
            mesh=mesh,
            in_specs=placed,
            out_specs=P("row", None),
            check_vma=False,
        )
        return mapped(snapshots, start_block)

    return run
```

```python
import functools
import math

import jax
import jax.numpy as jnp
from jax import lax
from jax.experimental import pallas as pl
from jax.experimental.pallas import tpu as pltpu
from jax.sharding import PartitionSpec as P


LAGS = 128
ITERS = 6
TILE = 128
PANEL = 16


kernel_spread = 0.25
highest = lax.Precision.HIGHEST
f32 = jnp.float32
bf16 = jnp.bfloat16


def broadcast(x, axis, root):
    mine = lax.axis_index(axis) == root
    return lax.psum(jnp.where(mine, x, jnp.zeros_like(x)), axis)


def shifted(x, axis, by):
    length = lax.axis_size(axis)
    pairs = [(i, i + by) for i in range(length) if 0 <= i + by < length]
    return lax.ppermute(x, axis, pairs)


def diagonal_window(extended, lag_count):
    running = None
    partial_sum = extended
    levels = lag_count.bit_length()
    for level in range(levels):
        stride = 1 << level
        if lag_count & stride:
            running = partial_sum
        if level + 1 < levels:
            partial_sum = partial_sum[:-stride, :-stride] + partial_sum[stride:, stride:]
    return running


def orthonormal(product, gram_sum):
    factor = jnp.linalg.cholesky(gram_sum)
    return jax.scipy.linalg.solve_triangular(factor, product.T, lower=True).T


def square_norms(fields):
    widened = fields.astype(f32)
    return jnp.sum(widened * widened, axis=1)


def spread_body(points, snapshots, start_block):
    row_total = lax.axis_size("row")
    col_total = lax.axis_size("col")
    row_place = lax.axis_index("row")
    col_place = lax.axis_index("col")
    shard_rows = snapshots.shape[0]
    block_rows = shard_rows * col_total
    pairing = row_total // col_total
    block_cols = block_rows * pairing
    own_rows = lax.all_gather(snapshots, "col", axis=0, tiled=True)
    own_norms = square_norms(own_rows)
    members = []
    for member in range(pairing):
        members.append(broadcast(own_rows, "row", pairing * col_place + member))
    col_data = jnp.concatenate(members, axis=0)
    col_norms = square_norms(col_data)
    products = lax.dot_general(
        own_rows, col_data, (((1,), (1,)), ((), ())), preferred_element_type=f32
    )
    partial_dist = own_norms[:, None] + col_norms[None, :] - 2.0 * products
    distance = lax.psum(partial_dist, "feat")
    rim_width = LAGS - 1
    top_rim = shifted(distance[block_rows - rim_width :], "row", 1)
    upper = jnp.concatenate([top_rim, distance], axis=0)
    left_side = shifted(upper[:, block_cols - rim_width :], "col", 1)
    extended = jnp.concatenate([left_side, upper], axis=1)
    lagged = diagonal_window(extended, LAGS)
    row_ids = row_place * block_rows + lax.broadcasted_iota(jnp.int32, (block_rows, block_cols), 0)
    col_ids = col_place * block_cols + lax.broadcasted_iota(jnp.int32, (block_rows, block_cols), 1)
    counts = jnp.minimum(jnp.minimum(row_ids, col_ids), rim_width) + 1
    kernel = jnp.exp(-(lagged / (counts.astype(f32) * points)) / kernel_spread)
    row_degree = lax.psum(jnp.sum(kernel, axis=1), "col")
    every_degree = lax.all_gather(row_degree, "row", axis=0, tiled=True)
    col_degree = lax.dynamic_slice_in_dim(every_degree, col_place * block_cols, block_cols)
    markov = kernel * lax.rsqrt(row_degree)[:, None] * lax.rsqrt(col_degree)[None, :]
    basis = start_block
    for _ in range(ITERS // 2):
        product = lax.dot_general(
            markov,
            basis,
            (((0,), (0,)), ((), ())),
            precision=highest,
            preferred_element_type=f32,
        )
        summed_cols = lax.psum(product, "row")
        row_product = jnp.dot(markov, summed_cols, precision=highest, preferred_element_type=f32)
        summed_rows = lax.psum(row_product, "col")
        local_gram = jnp.dot(
            summed_rows.T, summed_rows, precision=highest, preferred_element_type=f32
        )
        gram_rows = lax.psum(local_gram, "row")
        basis = orthonormal(summed_rows, gram_rows)
    return basis * math.sqrt(row_total * block_rows)


def any_spec():
    return pl.BlockSpec(memory_space=pl.ANY)


def vmem_spec():
    return pl.BlockSpec(memory_space=pltpu.VMEM)


def near(x):
    return pltpu.with_memory_space_constraint(x, pltpu.VMEM)


def xor_permute(x, axis, mask):
    return lax.ppermute(x, axis, [(i, i ^ mask) for i in range(lax.axis_size(axis))])


def quad_permute(x, mask):
    cols, feats = lax.axis_size("col"), lax.axis_size("feat")
    pairs = []
    for col in range(cols):
        for feat in range(feats):
            there = (col ^ (mask >> 1)) * feats + (feat ^ ((mask & 1) * (feats // 2)))
            pairs.append((col * feats + feat, there))
    return lax.ppermute(x, ("col", "feat"), pairs)


def packed_blocks(tiles):
    full = [(b, c) for b in range(tiles) for c in range(b)]
    return full, [(b, b + 1) for b in range(0, tiles, 2)]


def ring_steps(rows, cols):
    shifts = [rows // 2, 1, rows - 1]
    steps = [(a, (n + turn) % cols) for turn in range(cols) for n, a in enumerate(shifts)]
    return [(0, 0)] + steps + [(0, mask) for mask in range(1, cols)]


def device_places():
    row, col, feat = lax.axis_index("row"), lax.axis_index("col"), lax.axis_index("feat")
    return feat & 1, col * 2 + (feat >> 1), row, col


def cut_kernel(steps, rows_total, cols, width, x_ref, *refs):
    members = len(steps)
    outs, sems = refs[:members], refs[members]
    parts = sems.shape[0] // members
    rows_each = x_ref.shape[0] // parts
    _, _, row, col = device_places()
    copies = []
    for step, (shift, mask) in enumerate(steps):
        there = lax.rem(row + shift, rows_total) * cols + (col ^ mask)
        begin = pl.multiple_of(there * width, TILE)
        for part in range(parts):
            rows = slice(part * rows_each, (part + 1) * rows_each)
            copies.append(
                pltpu.make_async_copy(
                    x_ref.at[rows, pl.ds(begin, width)],
                    outs[step].at[rows, :],
                    sems.at[step * parts + part],
                )
            )
    for copy in copies:
        copy.start()
    for copy in copies:
        copy.wait()


def pieces_of(whole):
    high = whole.astype(bf16)
    rest = whole - high.astype(f32)
    middle = rest.astype(bf16)
    return high, middle, (rest - middle.astype(f32)).astype(bf16)


def add_dots(weights, pieces):
    total = None
    for piece in pieces:
        term = jnp.dot(weights, piece, preferred_element_type=f32)
        total = term if total is None else total + term
    return total


def gram_kernel(steps, rows_total, cols, rows, *refs):
    members = len(steps)
    received, starts = refs[:members], refs[members : members + 2]
    keep_ref, send_ref, begin_ref, data_ref = refs[members + 2 :]
    half, _, row_place, col_place = device_places()
    for step, (shift, mask) in enumerate(steps):
        source = lax.rem(row_place + (rows_total - shift), rows_total) * cols + (col_place ^ mask)
        data_ref[pl.ds(pl.multiple_of(source * rows, rows), rows), :] = received[step][...]
    vecs = starts[0].shape[0]
    for mask in range(2):
        begin_ref[mask * vecs : (mask + 1) * vecs, :] = starts[mask][...]
    tiles = members * rows // TILE
    sub = lax.broadcasted_iota(jnp.int32, (TILE, TILE), 0)
    lane = lax.broadcasted_iota(jnp.int32, (TILE, TILE), 1)
    anti = sub + lane == TILE - 1
    flip = anti.astype(bf16)
    contract = (((1,), (1,)), ((), ()))
    strips, row_norms, col_norms = [], [], []
    for b in range(tiles):
        mirror = tiles - 1 - b
        block = data_ref[mirror * TILE : (mirror + 1) * TILE, :]
        turned = jnp.dot(flip, block, preferred_element_type=f32).astype(bf16)
        prods = lax.dot_general(
            turned, data_ref[: (mirror + 1) * TILE, :], contract, preferred_element_type=f32
        )
        strips.append(prods)
        own = jnp.where(anti, prods[:, mirror * TILE :], 0.0)
        row_norms.append(jnp.sum(own, axis=1, keepdims=True))
        col_norms.append(jnp.sum(own, axis=0, keepdims=True))
    norms = jnp.concatenate(col_norms[::-1], axis=1)
    late = (sub + lane >= TILE - 1).astype(bf16)
    early = (sub + lane < TILE - 1).astype(bf16)
    skewed = []
    for b in range(tiles):
        span = (tiles - b) * TILE
        dist = row_norms[b] + norms[:, :span] - 2.0 * strips[b]
        dist = pltpu.roll(dist, 0, 1, stride=1, stride_axis=0)
        head = jnp.where(lane >= sub, dist[:, :TILE], 0.0)
        if span > TILE:
            head = jnp.concatenate([head, dist[:, TILE:]], axis=1)
        skewed.append(pieces_of(head))
    lags = []
    for block in range(tiles):
        b = tiles - 1 - block
        span = (block + 1) * TILE
        lagged = add_dots(late, skewed[b])
        if block > 0:
            more = add_dots(early, skewed[b + 1])
            lagged = jnp.concatenate([lagged[:, :TILE], lagged[:, TILE:] + more], axis=1)
        lags.append(pltpu.roll(lagged, (1 + span - TILE) % span, 1, stride=1, stride_axis=0))
    full, pairs = packed_blocks(tiles)
    values = [lags[b][:, c * TILE : (c + 1) * TILE] for b, c in full]
    for one, two in pairs:
        values.append(jnp.where(lane < sub, lags[one][:, -TILE:], lags[two][:, -TILE:].T))
    count = len(values) // 2
    for slot in range(count):
        rows = slice(slot * TILE, (slot + 1) * TILE)
        keep_ref[rows, :] = jnp.where(half == 0, values[slot], values[count + slot])
        send_ref[rows, :] = jnp.where(half == 0, values[count + slot], values[slot])


def quarter_kernel(chunk, keep_ref, got_ref, *outs):
    quad = device_places()[1]
    for mask in range(4):
        rows = pl.ds(pl.multiple_of((quad ^ mask) * chunk, 8), chunk)
        outs[mask][...] = keep_ref[rows, :] + got_ref[rows, :]


def split(x):
    high = x.astype(bf16)
    return high, (x - high.astype(f32)).astype(bf16)


def split_dot(a, b, contract=(((1,), (0,)), ((), ()))):
    a_high, a_low = split(a)
    b_high, b_low = split(b)
    rows = a.shape[0]
    stacked = jnp.concatenate([a_high, a_low], axis=0)
    first = lax.dot_general(stacked, b_high, contract, preferred_element_type=f32)
    second = lax.dot_general(a_high, b_low, contract, preferred_element_type=f32)
    return first[:rows] + (first[rows:] + second)


def inverse_factor(small):
    size = small.shape[0]
    sub = lax.broadcasted_iota(jnp.int32, (size, size), 0)
    lane = lax.broadcasted_iota(jnp.int32, (size, size), 1)
    eye = (sub == lane).astype(f32)
    rest = jnp.concatenate([small, eye], axis=1)
    done = []
    for first in range(0, size, PANEL):
        wide = rest.shape
        below = lax.broadcasted_iota(jnp.int32, wide, 0)
        columns = [
            jnp.broadcast_to(rest[:, first + a : first + a + 1], wide) for a in range(PANEL)
        ]
        for a in range(min(PANEL, size - 1 - first)):
            scale = columns[a] * (1.0 / columns[a][a : a + 1, :])
            scale = jnp.where(below > a, scale, 0.0)
            for b in range(a + 1, PANEL):
                columns[b] = columns[b] - scale * columns[b][a : a + 1, :]
            rest = rest - scale * rest[a : a + 1, :]
        done.append(rest[:PANEL, :])
        rest = rest[PANEL:, :]
    work = jnp.concatenate(done, axis=0)
    pivots = jnp.sum(work[:, :size] * eye, axis=1, keepdims=True)
    begin = jnp.sum(small * eye, axis=1, keepdims=True)
    return work[:, size:] * lax.rsqrt(pivots), jnp.min(pivots / begin)


def finish_kernel(points, tiles, chunk, snaps, *refs):
    pieces, begins = refs[:8], refs[8:10]
    out_ref, packed_ref, high_ref, low_ref, wide_ref = refs[10:]
    half, quad, row_place, _ = device_places()
    for side in range(2):
        for mask in range(4):
            begin = pl.multiple_of((half ^ side) * (4 * chunk) + (quad ^ mask) * chunk, 8)
            packed_ref[pl.ds(begin, chunk), :] = pieces[side * 4 + mask][...]
    rows = snaps // 4
    sub = lax.broadcasted_iota(jnp.int32, (TILE, TILE), 0)
    lane = lax.broadcasted_iota(jnp.int32, (TILE, TILE), 1)
    full, pairs = packed_blocks(tiles)

    def factor(counts):
        return -1.0 / (counts.astype(f32) * (points * kernel_spread))

    def keep(value, block, c):
        high, low = split(value)
        high_ref[block * TILE : (block + 1) * TILE, c * TILE : (c + 1) * TILE] = high
        low_ref[block * TILE : (block + 1) * TILE, c * TILE : (c + 1) * TILE] = low

    for at, (block, c) in enumerate(full):
        columns = c * TILE + lane[:1, :]
        scale = factor(jnp.minimum(columns, LAGS - 1) + 1)
        value = jnp.exp(packed_ref[at * TILE : (at + 1) * TILE, :] * scale)
        keep(value, block, c)
        keep(value.T, c, block)
    for at, (one, two) in enumerate(pairs):
        shared = packed_ref[(len(full) + at) * TILE : (len(full) + at + 1) * TILE, :]
        swapped = shared.T
        for block, lagged in (
            (one, jnp.where(lane < sub, shared, swapped)),
            (two, jnp.where(lane > sub, shared, swapped)),
        ):
            counts = jnp.minimum(block * TILE + jnp.minimum(sub, lane), LAGS - 1) + 1
            lagged = jnp.where(lane == sub, 0.0, lagged)
            keep(jnp.exp(lagged * factor(counts)), block, block)
    rows_sum = jnp.zeros((8, snaps), f32)
    for block in range(0, snaps, 64):
        both = slice(block, block + 64)
        part = high_ref[both, :].astype(f32) + low_ref[both, :].astype(f32)
        for at in range(0, 64, 8):
            rows_sum = rows_sum + part[at : at + 8, :]
    inverse = 1.0 / jnp.sum(rows_sum, axis=0, keepdims=True)
    scales = lax.sqrt(inverse)
    vecs = begins[0].shape[0] // 2
    for mask in range(4):
        begin = pl.multiple_of((row_place ^ mask) * rows, TILE)
        half_rows = slice(mask % 2 * vecs, (mask % 2 + 1) * vecs)
        wide_ref[:, pl.ds(begin, rows)] = begins[mask // 2][half_rows, :]
    start = wide_ref[...]

    def apply(x):
        x_high, x_low = split(x)
        stacked = jnp.concatenate([x_high, x_low], axis=0)
        first = jnp.dot(stacked, high_ref[...], preferred_element_type=f32)
        second = jnp.dot(x_high, low_ref[...], preferred_element_type=f32)
        return first[:vecs] + (first[vecs:] + second)

    across = (((1,), (1,)), ((), ()))

    def rounds(x, least, times):
        x = apply(x * scales)
        for _ in range(times - 1):
            x = apply(x * inverse)
        x = x * scales
        factor, ratio = inverse_factor(split_dot(x, x, across))
        return split_dot(factor, x), jnp.minimum(least, ratio)

    def loop(times):
        return lax.fori_loop(
            0,
            ITERS // times,
            lambda _, c: rounds(c[0], c[1], times),
            (start, f32(1.0)),
            unroll=times == 3,
        )

    basis, least = loop(3)
    wide_ref[...] = basis

    @pl.when(jnp.logical_not(least > 1e-4))
    def _():
        wide_ref[...] = loop(1)[0]

    basis = wide_ref[...]
    eye_sub = lax.broadcasted_iota(jnp.int32, (vecs, vecs), 0)
    eye_lane = lax.broadcasted_iota(jnp.int32, (vecs, vecs), 1)
    error = split_dot(basis, basis, across) - (eye_sub == eye_lane).astype(f32)
    weight = jnp.where(eye_sub > eye_lane, 1.0, jnp.where(eye_sub == eye_lane, 0.5, 0.0))
    wide_ref[...] = (basis - split_dot(error * weight, basis)) * math.sqrt(snaps)
    out_ref[...] = wide_ref[:, pl.ds(pl.multiple_of(row_place * rows, TILE), rows)]


def packed_body(points, snapshots, start_block):
    return packed_plan(points, snapshots, start_block)


def packed_plan(points, snapshots, start_block):
    cols = lax.axis_size("col")
    rows_total = lax.axis_size("row")
    members = rows_total * cols
    shard_rows, shard_points = snapshots.shape
    width = shard_points // members
    snaps = shard_rows * members
    tiles = snaps // TILE
    vecs = start_block.shape[1]
    steps = ring_steps(rows_total, cols)
    cuts = {}
    for group in ((1,), tuple(range(2, members)) + (0,)):
        chosen = [steps[step] for step in group]
        outs = pl.pallas_call(
            functools.partial(cut_kernel, chosen, rows_total, cols, width),
            out_shape=[pltpu.VMEM((shard_rows, width), bf16)] * len(group),
            in_specs=[any_spec()],
            out_specs=[vmem_spec()] * len(group),
            scratch_shapes=[pltpu.SemaphoreType.DMA((len(group) * (4 if len(group) == 1 else 1),))],
            name="cut",
        )(snapshots)
        cuts.update(zip(group, outs))
    received = [cuts[0]]
    for step in range(1, members):
        shift, mask = steps[step]
        pairs = []
        for row in range(rows_total):
            for col in range(cols):
                there = (row + shift) % rows_total * cols + (col ^ mask)
                pairs.append((row * cols + col, there))
        received.append(lax.ppermute(cuts[step], ("row", "col"), pairs))
    turned = start_block.T
    starts = [turned, xor_permute(turned, "row", 1)]

    full, shared = packed_blocks(tiles)
    total = (len(full) + len(shared)) * TILE
    side = total // 2
    chunk = side // 4
    keep, send, begin = pl.pallas_call(
        functools.partial(gram_kernel, steps, rows_total, cols, shard_rows),
        out_shape=[pltpu.VMEM((side, TILE), f32)] * 2 + [pltpu.VMEM((2 * vecs, snaps // rows_total), f32)],
        in_specs=[vmem_spec()] * (members + 2),
        out_specs=[vmem_spec()] * 3,
        scratch_shapes=[pltpu.VMEM((snaps, width), bf16)],
        name="gram",
    )(*[near(x) for x in received + starts])
    got = xor_permute(send, "feat", 1)
    begins = [begin, xor_permute(begin, "row", 2)]
    quarters = pl.pallas_call(
        functools.partial(quarter_kernel, chunk),
        out_shape=[pltpu.VMEM((chunk, TILE), f32)] * 4,
        in_specs=[vmem_spec()] * 2,
        out_specs=[vmem_spec()] * 4,
        name="quarter",
    )(near(keep), near(got))
    mine = quarters[0]
    arrived = {}
    for mask in (3, 1, 2):
        arrived[mask] = quad_permute(quarters[mask], mask)
    mine = (mine + arrived[3]) + (arrived[1] + arrived[2])
    others = {mask: xor_permute(mine, "row", mask) for mask in (1, 3, 2)}
    mine = (mine + others[1]) + (others[3] + others[2])
    pieces = [mine] + [quad_permute(mine, mask) for mask in range(1, 4)]
    pieces = pieces + [xor_permute(piece, "feat", 1) for piece in pieces]
    basis = pl.pallas_call(
        functools.partial(finish_kernel, float(points), tiles, chunk, snaps),
        out_shape=jax.ShapeDtypeStruct((vecs, snaps // rows_total), f32),
        in_specs=[vmem_spec()] * 10,
        out_specs=vmem_spec(),
        scratch_shapes=[
            pltpu.VMEM((total, TILE), f32),
            pltpu.VMEM((snaps, snaps), bf16),
            pltpu.VMEM((snaps, snaps), bf16),
            pltpu.VMEM((vecs, snaps), f32),
        ],
        name="finish",
    )(*[near(x) for x in pieces + begins])
    return basis.T


def solution(mesh):
    sizes = dict(mesh.shape)
    placed = (P(("row", "col"), "feat"), P("row", None))

    def run(snapshots, start_block):
        snaps, points = snapshots.shape
        members = sizes["row"] * sizes["col"]
        tiles = snaps // TILE
        packs = (
            sizes["row"] == 4
            and sizes["col"] == 2
            and sizes["feat"] == 4
            and snaps % (TILE * sizes["row"]) == 0
            and points % (TILE * members * sizes["feat"]) == 0
            and (tiles * tiles // 2) % 2 == 0
            and snaps <= 1024
        )
        body = packed_body if packs else spread_body
        mapped = jax.shard_map(
            functools.partial(body, points),
            mesh=mesh,
            in_specs=placed,
            out_specs=P("row", None),
            check_vma=False,
        )
        return mapped(snapshots, start_block)

    return run
```

```python
import functools
import math

import jax
import jax.numpy as jnp
from jax import lax
from jax.experimental import pallas as pl
from jax.experimental.pallas import tpu as pltpu
from jax.sharding import PartitionSpec as P


LAGS = 128
ITERS = 6
TILE = 128
PANEL = 16


kernel_spread = 0.25
highest = lax.Precision.HIGHEST
f32 = jnp.float32
bf16 = jnp.bfloat16


def broadcast(x, axis, root):
    mine = lax.axis_index(axis) == root
    return lax.psum(jnp.where(mine, x, jnp.zeros_like(x)), axis)


def shifted(x, axis, by):
    length = lax.axis_size(axis)
    pairs = [(i, i + by) for i in range(length) if 0 <= i + by < length]
    return lax.ppermute(x, axis, pairs)


def diagonal_window(extended, lag_count):
    running = None
    partial_sum = extended
    levels = lag_count.bit_length()
    for level in range(levels):
        stride = 1 << level
        if lag_count & stride:
            running = partial_sum
        if level + 1 < levels:
            partial_sum = partial_sum[:-stride, :-stride] + partial_sum[stride:, stride:]
    return running


def orthonormal(product, gram_sum):
    factor = jnp.linalg.cholesky(gram_sum)
    return jax.scipy.linalg.solve_triangular(factor, product.T, lower=True).T


def square_norms(fields):
    widened = fields.astype(f32)
    return jnp.sum(widened * widened, axis=1)


def spread_body(points, snapshots, start_block):
    row_total = lax.axis_size("row")
    col_total = lax.axis_size("col")
    row_place = lax.axis_index("row")
    col_place = lax.axis_index("col")
    shard_rows = snapshots.shape[0]
    block_rows = shard_rows * col_total
    pairing = row_total // col_total
    block_cols = block_rows * pairing
    own_rows = lax.all_gather(snapshots, "col", axis=0, tiled=True)
    own_norms = square_norms(own_rows)
    members = []
    for member in range(pairing):
        members.append(broadcast(own_rows, "row", pairing * col_place + member))
    col_data = jnp.concatenate(members, axis=0)
    col_norms = square_norms(col_data)
    products = lax.dot_general(
        own_rows, col_data, (((1,), (1,)), ((), ())), preferred_element_type=f32
    )
    partial_dist = own_norms[:, None] + col_norms[None, :] - 2.0 * products
    distance = lax.psum(partial_dist, "feat")
    rim_width = LAGS - 1
    top_rim = shifted(distance[block_rows - rim_width :], "row", 1)
    upper = jnp.concatenate([top_rim, distance], axis=0)
    left_side = shifted(upper[:, block_cols - rim_width :], "col", 1)
    extended = jnp.concatenate([left_side, upper], axis=1)
    lagged = diagonal_window(extended, LAGS)
    row_ids = row_place * block_rows + lax.broadcasted_iota(jnp.int32, (block_rows, block_cols), 0)
    col_ids = col_place * block_cols + lax.broadcasted_iota(jnp.int32, (block_rows, block_cols), 1)
    counts = jnp.minimum(jnp.minimum(row_ids, col_ids), rim_width) + 1
    kernel = jnp.exp(-(lagged / (counts.astype(f32) * points)) / kernel_spread)
    row_degree = lax.psum(jnp.sum(kernel, axis=1), "col")
    every_degree = lax.all_gather(row_degree, "row", axis=0, tiled=True)
    col_degree = lax.dynamic_slice_in_dim(every_degree, col_place * block_cols, block_cols)
    markov = kernel * lax.rsqrt(row_degree)[:, None] * lax.rsqrt(col_degree)[None, :]
    basis = start_block
    for _ in range(ITERS // 2):
        product = lax.dot_general(
            markov,
            basis,
            (((0,), (0,)), ((), ())),
            precision=highest,
            preferred_element_type=f32,
        )
        summed_cols = lax.psum(product, "row")
        row_product = jnp.dot(markov, summed_cols, precision=highest, preferred_element_type=f32)
        summed_rows = lax.psum(row_product, "col")
        local_gram = jnp.dot(
            summed_rows.T, summed_rows, precision=highest, preferred_element_type=f32
        )
        gram_rows = lax.psum(local_gram, "row")
        basis = orthonormal(summed_rows, gram_rows)
    return basis * math.sqrt(row_total * block_rows)


def any_spec():
    return pl.BlockSpec(memory_space=pl.ANY)


def vmem_spec():
    return pl.BlockSpec(memory_space=pltpu.VMEM)


def near(x):
    return pltpu.with_memory_space_constraint(x, pltpu.VMEM)


def xor_permute(x, axis, mask):
    return lax.ppermute(x, axis, [(i, i ^ mask) for i in range(lax.axis_size(axis))])


def quad_permute(x, mask):
    cols, feats = lax.axis_size("col"), lax.axis_size("feat")
    pairs = []
    for col in range(cols):
        for feat in range(feats):
            there = (col ^ (mask >> 1)) * feats + (feat ^ ((mask & 1) * (feats // 2)))
            pairs.append((col * feats + feat, there))
    return lax.ppermute(x, ("col", "feat"), pairs)


def packed_blocks(tiles):
    full = [(b, c) for b in range(tiles) for c in range(b)]
    return full, [(b, b + 1) for b in range(0, tiles, 2)]


def ring_steps(rows, cols):
    shifts = [rows // 2, 1, rows - 1]
    steps = [(a, (n + turn) % cols) for turn in range(cols) for n, a in enumerate(shifts)]
    return [(0, 0)] + steps + [(0, mask) for mask in range(1, cols)]


def device_places():
    row, col, feat = lax.axis_index("row"), lax.axis_index("col"), lax.axis_index("feat")
    return feat & 1, col * 2 + (feat >> 1), row, col


def cut_kernel(steps, rows_total, cols, width, x_ref, *refs):
    members = len(steps)
    outs, sems = refs[:members], refs[members]
    parts = sems.shape[0] // members
    rows_each = x_ref.shape[0] // parts
    _, _, row, col = device_places()
    copies = []
    for step, (shift, mask) in enumerate(steps):
        there = lax.rem(row + shift, rows_total) * cols + (col ^ mask)
        begin = pl.multiple_of(there * width, TILE)
        for part in range(parts):
            rows = slice(part * rows_each, (part + 1) * rows_each)
            copies.append(
                pltpu.make_async_copy(
                    x_ref.at[rows, pl.ds(begin, width)],
                    outs[step].at[rows, :],
                    sems.at[step * parts + part],
                )
            )
    for copy in copies:
        copy.start()
    for copy in copies:
        copy.wait()


def pieces_of(whole):
    high = whole.astype(bf16)
    rest = whole - high.astype(f32)
    middle = rest.astype(bf16)
    return high, middle, (rest - middle.astype(f32)).astype(bf16)


def add_dots(weights, pieces):
    total = None
    for piece in pieces:
        term = jnp.dot(weights, piece, preferred_element_type=f32)
        total = term if total is None else total + term
    return total


def gram_kernel(steps, rows_total, cols, rows, *refs):
    members = len(steps)
    received, starts = refs[:members], refs[members : members + 2]
    keep_ref, send_ref, begin_ref, data_ref = refs[members + 2 :]
    half, _, row_place, col_place = device_places()
    for step, (shift, mask) in enumerate(steps):
        source = lax.rem(row_place + (rows_total - shift), rows_total) * cols + (col_place ^ mask)
        data_ref[pl.ds(pl.multiple_of(source * rows, rows), rows), :] = received[step][...]
    vecs = starts[0].shape[0]
    for mask in range(2):
        begin_ref[mask * vecs : (mask + 1) * vecs, :] = starts[mask][...]
    tiles = members * rows // TILE
    sub = lax.broadcasted_iota(jnp.int32, (TILE, TILE), 0)
    lane = lax.broadcasted_iota(jnp.int32, (TILE, TILE), 1)
    anti = sub + lane == TILE - 1
    flip = anti.astype(bf16)
    contract = (((1,), (1,)), ((), ()))
    strips, row_norms, col_norms = [], [], []
    for b in range(tiles):
        mirror = tiles - 1 - b
        block = data_ref[mirror * TILE : (mirror + 1) * TILE, :]
        turned = jnp.dot(flip, block, preferred_element_type=f32).astype(bf16)
        prods = lax.dot_general(
            turned, data_ref[: (mirror + 1) * TILE, :], contract, preferred_element_type=f32
        )
        strips.append(prods)
        own = jnp.where(anti, prods[:, mirror * TILE :], 0.0)
        row_norms.append(jnp.sum(own, axis=1, keepdims=True))
        col_norms.append(jnp.sum(own, axis=0, keepdims=True))
    norms = jnp.concatenate(col_norms[::-1], axis=1)
    late = (sub + lane >= TILE - 1).astype(bf16)
    early = (sub + lane < TILE - 1).astype(bf16)
    skewed = []
    for b in range(tiles):
        span = (tiles - b) * TILE
        dist = row_norms[b] + norms[:, :span] - 2.0 * strips[b]
        dist = pltpu.roll(dist, 0, 1, stride=1, stride_axis=0)
        head = jnp.where(lane >= sub, dist[:, :TILE], 0.0)
        if span > TILE:
            head = jnp.concatenate([head, dist[:, TILE:]], axis=1)
        skewed.append(pieces_of(head))
    lags = []
    for block in range(tiles):
        b = tiles - 1 - block
        span = (block + 1) * TILE
        lagged = add_dots(late, skewed[b])
        if block > 0:
            more = add_dots(early, skewed[b + 1])
            lagged = jnp.concatenate([lagged[:, :TILE], lagged[:, TILE:] + more], axis=1)
        lags.append(pltpu.roll(lagged, (1 + span - TILE) % span, 1, stride=1, stride_axis=0))
    full, pairs = packed_blocks(tiles)
    values = [lags[b][:, c * TILE : (c + 1) * TILE] for b, c in full]
    for one, two in pairs:
        values.append(jnp.where(lane < sub, lags[one][:, -TILE:], lags[two][:, -TILE:].T))
    count = len(values) // 2
    for slot in range(count):
        rows = slice(slot * TILE, (slot + 1) * TILE)
        keep_ref[rows, :] = jnp.where(half == 0, values[slot], values[count + slot])
        send_ref[rows, :] = jnp.where(half == 0, values[count + slot], values[slot])


def quarter_kernel(chunk, keep_ref, got_ref, *outs):
    quad = device_places()[1]
    for mask in range(4):
        rows = pl.ds(pl.multiple_of((quad ^ mask) * chunk, 8), chunk)
        outs[mask][...] = keep_ref[rows, :] + got_ref[rows, :]


def split(x):
    high = x.astype(bf16)
    return high, (x - high.astype(f32)).astype(bf16)


def split_dot(a, b, contract=(((1,), (0,)), ((), ()))):
    a_high, a_low = split(a)
    b_high, b_low = split(b)
    rows = a.shape[0]
    stacked = jnp.concatenate([a_high, a_low], axis=0)
    first = lax.dot_general(stacked, b_high, contract, preferred_element_type=f32)
    second = lax.dot_general(a_high, b_low, contract, preferred_element_type=f32)
    return first[:rows] + (first[rows:] + second)


def inverse_factor(small):
    size = small.shape[0]
    sub = lax.broadcasted_iota(jnp.int32, (size, size), 0)
    lane = lax.broadcasted_iota(jnp.int32, (size, size), 1)
    eye = (sub == lane).astype(f32)
    rest = jnp.concatenate([small, eye], axis=1)
    done = []
    for first in range(0, size, PANEL):
        wide = rest.shape
        below = lax.broadcasted_iota(jnp.int32, wide, 0)
        columns = [
            jnp.broadcast_to(rest[:, first + a : first + a + 1], wide) for a in range(PANEL)
        ]
        for a in range(min(PANEL, size - 1 - first)):
            scale = columns[a] * (1.0 / columns[a][a : a + 1, :])
            scale = jnp.where(below > a, scale, 0.0)
            for b in range(a + 1, PANEL):
                columns[b] = columns[b] - scale * columns[b][a : a + 1, :]
            rest = rest - scale * rest[a : a + 1, :]
        done.append(rest[:PANEL, :])
        rest = rest[PANEL:, :]
    work = jnp.concatenate(done, axis=0)
    pivots = jnp.sum(work[:, :size] * eye, axis=1, keepdims=True)
    begin = jnp.sum(small * eye, axis=1, keepdims=True)
    return work[:, size:] * lax.rsqrt(pivots), jnp.min(pivots / begin)


def finish_kernel(points, tiles, chunk, snaps, *refs):
    pieces, begins = refs[:8], refs[8:10]
    out_ref, packed_ref, high_ref, low_ref, wide_ref = refs[10:]
    half, quad, row_place, _ = device_places()
    for side in range(2):
        for mask in range(4):
            begin = pl.multiple_of((half ^ side) * (4 * chunk) + (quad ^ mask) * chunk, 8)
            packed_ref[pl.ds(begin, chunk), :] = pieces[side * 4 + mask][...]
    rows = snaps // 4
    sub = lax.broadcasted_iota(jnp.int32, (TILE, TILE), 0)
    lane = lax.broadcasted_iota(jnp.int32, (TILE, TILE), 1)
    full, pairs = packed_blocks(tiles)

    def factor(counts):
        return -1.0 / (counts.astype(f32) * (points * kernel_spread))

    def keep(value, block, c):
        high, low = split(value)
        high_ref[block * TILE : (block + 1) * TILE, c * TILE : (c + 1) * TILE] = high
        low_ref[block * TILE : (block + 1) * TILE, c * TILE : (c + 1) * TILE] = low

    for at, (block, c) in enumerate(full):
        columns = c * TILE + lane[:1, :]
        scale = factor(jnp.minimum(columns, LAGS - 1) + 1)
        value = jnp.exp(packed_ref[at * TILE : (at + 1) * TILE, :] * scale)
        keep(value, block, c)
        keep(value.T, c, block)
    for at, (one, two) in enumerate(pairs):
        shared = packed_ref[(len(full) + at) * TILE : (len(full) + at + 1) * TILE, :]
        swapped = shared.T
        for block, lagged in (
            (one, jnp.where(lane < sub, shared, swapped)),
            (two, jnp.where(lane > sub, shared, swapped)),
        ):
            counts = jnp.minimum(block * TILE + jnp.minimum(sub, lane), LAGS - 1) + 1
            lagged = jnp.where(lane == sub, 0.0, lagged)
            keep(jnp.exp(lagged * factor(counts)), block, block)
    rows_sum = jnp.zeros((8, snaps), f32)
    for block in range(0, snaps, 64):
        both = slice(block, block + 64)
        part = high_ref[both, :].astype(f32) + low_ref[both, :].astype(f32)
        for at in range(0, 64, 8):
            rows_sum = rows_sum + part[at : at + 8, :]
    inverse = 1.0 / jnp.sum(rows_sum, axis=0, keepdims=True)
    scales = lax.sqrt(inverse)
    vecs = begins[0].shape[0] // 2
    for mask in range(4):
        begin = pl.multiple_of((row_place ^ mask) * rows, TILE)
        half_rows = slice(mask % 2 * vecs, (mask % 2 + 1) * vecs)
        wide_ref[:, pl.ds(begin, rows)] = begins[mask // 2][half_rows, :]
    start = wide_ref[...]

    def apply(x):
        x_high, x_low = split(x)
        stacked = jnp.concatenate([x_high, x_low], axis=0)
        first = jnp.dot(stacked, high_ref[...], preferred_element_type=f32)
        second = jnp.dot(x_high, low_ref[...], preferred_element_type=f32)
        return first[:vecs] + (first[vecs:] + second)

    across = (((1,), (1,)), ((), ()))

    def rounds(x, least, times):
        x = apply(x * scales)
        for _ in range(times - 1):
            x = apply(x * inverse)
        x = x * scales
        factor, ratio = inverse_factor(split_dot(x, x, across))
        return split_dot(factor, x), jnp.minimum(least, ratio)

    def loop(times):
        return lax.fori_loop(
            0,
            ITERS // times,
            lambda _, c: rounds(c[0], c[1], times),
            (start, f32(1.0)),
            unroll=times == 3,
        )

    basis, least = loop(3)
    wide_ref[...] = basis

    @pl.when(jnp.logical_not(least > 1e-4))
    def _():
        wide_ref[...] = loop(1)[0]

    basis = wide_ref[...]
    eye_sub = lax.broadcasted_iota(jnp.int32, (vecs, vecs), 0)
    eye_lane = lax.broadcasted_iota(jnp.int32, (vecs, vecs), 1)
    error = split_dot(basis, basis, across) - (eye_sub == eye_lane).astype(f32)
    weight = jnp.where(eye_sub > eye_lane, 1.0, jnp.where(eye_sub == eye_lane, 0.5, 0.0))
    fix = jnp.dot(
        (error * weight).astype(bf16), basis.astype(bf16), preferred_element_type=f32
    )
    wide_ref[...] = (basis - fix) * math.sqrt(snaps)
    out_ref[...] = wide_ref[:, pl.ds(pl.multiple_of(row_place * rows, TILE), rows)]


def packed_body(points, snapshots, start_block):
    return packed_plan(points, snapshots, start_block)


def packed_plan(points, snapshots, start_block):
    cols = lax.axis_size("col")
    rows_total = lax.axis_size("row")
    members = rows_total * cols
    shard_rows, shard_points = snapshots.shape
    width = shard_points // members
    snaps = shard_rows * members
    tiles = snaps // TILE
    vecs = start_block.shape[1]
    steps = ring_steps(rows_total, cols)
    cuts = {}
    for group in ((1,), tuple(range(2, members)) + (0,)):
        chosen = [steps[step] for step in group]
        outs = pl.pallas_call(
            functools.partial(cut_kernel, chosen, rows_total, cols, width),
            out_shape=[pltpu.VMEM((shard_rows, width), bf16)] * len(group),
            in_specs=[any_spec()],
            out_specs=[vmem_spec()] * len(group),
            scratch_shapes=[pltpu.SemaphoreType.DMA((len(group) * (4 if len(group) == 1 else 1),))],
            name="cut",
        )(snapshots)
        cuts.update(zip(group, outs))
    received = [cuts[0]]
    for step in range(1, members):
        shift, mask = steps[step]
        pairs = []
        for row in range(rows_total):
            for col in range(cols):
                there = (row + shift) % rows_total * cols + (col ^ mask)
                pairs.append((row * cols + col, there))
        received.append(lax.ppermute(cuts[step], ("row", "col"), pairs))
    turned = start_block.T
    starts = [turned, xor_permute(turned, "row", 1)]

    full, shared = packed_blocks(tiles)
    total = (len(full) + len(shared)) * TILE
    side = total // 2
    chunk = side // 4
    keep, send, begin = pl.pallas_call(
        functools.partial(gram_kernel, steps, rows_total, cols, shard_rows),
        out_shape=[pltpu.VMEM((side, TILE), f32)] * 2 + [pltpu.VMEM((2 * vecs, snaps // rows_total), f32)],
        in_specs=[vmem_spec()] * (members + 2),
        out_specs=[vmem_spec()] * 3,
        scratch_shapes=[pltpu.VMEM((snaps, width), bf16)],
        name="gram",
    )(*[near(x) for x in received + starts])
    got = xor_permute(send, "feat", 1)
    begins = [begin, xor_permute(begin, "row", 2)]
    quarters = pl.pallas_call(
        functools.partial(quarter_kernel, chunk),
        out_shape=[pltpu.VMEM((chunk, TILE), f32)] * 4,
        in_specs=[vmem_spec()] * 2,
        out_specs=[vmem_spec()] * 4,
        name="quarter",
    )(near(keep), near(got))
    mine = quarters[0]
    arrived = {}
    for mask in (3, 1, 2):
        arrived[mask] = quad_permute(quarters[mask], mask)
    mine = (mine + arrived[3]) + (arrived[1] + arrived[2])
    others = {mask: xor_permute(mine, "row", mask) for mask in (1, 3, 2)}
    mine = (mine + others[1]) + (others[3] + others[2])
    pieces = [mine] + [quad_permute(mine, mask) for mask in range(1, 4)]
    pieces = pieces + [xor_permute(piece, "feat", 1) for piece in pieces]
    basis = pl.pallas_call(
        functools.partial(finish_kernel, float(points), tiles, chunk, snaps),
        out_shape=jax.ShapeDtypeStruct((vecs, snaps // rows_total), f32),
        in_specs=[vmem_spec()] * 10,
        out_specs=vmem_spec(),
        scratch_shapes=[
            pltpu.VMEM((total, TILE), f32),
            pltpu.VMEM((snaps, snaps), bf16),
            pltpu.VMEM((snaps, snaps), bf16),
            pltpu.VMEM((vecs, snaps), f32),
        ],
        name="finish",
    )(*[near(x) for x in pieces + begins])
    return basis.T


def solution(mesh):
    sizes = dict(mesh.shape)
    placed = (P(("row", "col"), "feat"), P("row", None))

    def run(snapshots, start_block):
        snaps, points = snapshots.shape
        members = sizes["row"] * sizes["col"]
        tiles = snaps // TILE
        packs = (
            sizes["row"] == 4
            and sizes["col"] == 2
            and sizes["feat"] == 4
            and snaps % (TILE * sizes["row"]) == 0
            and points % (TILE * members * sizes["feat"]) == 0
            and (tiles * tiles // 2) % 2 == 0
            and snaps <= 1024
        )
        body = packed_body if packs else spread_body
        mapped = jax.shard_map(
            functools.partial(body, points),
            mesh=mesh,
            in_specs=placed,
            out_specs=P("row", None),
            check_vma=False,
        )
        return mapped(snapshots, start_block)

    return run
```
